32 devices in a mesh: grp: 2 (over x), frame: 8 (over z, y), row: 2 (over core).
Axes of the slice: x: 2, y: 2, z: 4, core: 2. Of those that a mesh axis runs over, the one named last changes fastest.
Arguments:
- latents: float32 [4, 8, 16, 32, 16], P('grp', 'frame', 'row'), parts along dimension 0, may hold values from -6 to 6
- target_noise: float32 [4, 8, 16, 32, 16], P('grp', 'frame', 'row'), parts along dimension 0, may hold values from -6 to 6
- timesteps: int32 [4], P('grp'), parts along dimension 0, may hold values from 0 to 999
- patch_weight: bfloat16 [16, 1152], replicated, may hold values from -1.5 to 1.5
- time_weight: bfloat16 [256, 1152], replicated, may hold values from -0.5 to 0.5
- spatial_project: bfloat16 [1152, 1728], replicated
- spatial_output: bfloat16 [576, 1152], replicated, may hold values from -0.75 to 0.75
- temporal_project: bfloat16 [1152, 1728], replicated
- temporal_output: bfloat16 [576, 1152], replicated, may hold values from -0.75 to 0.75
- final_weight: bfloat16 [1152, 16], replicated, may hold values from -0.1875 to 0.1875
Outputs:
- errors: float32 [4, 8, 16, 32], P('grp', 'frame', 'row'), parts along dimension 0
The draws below stay inside these ranges and needn't reach their ends.
There are 2 independent parts, one for each index of `grp`. The reference program is written for one: setup_inputs(seed, part) draws one part's arguments, and reference() takes and returns one part's arrays. A program takes and returns all parts, laid end to end along the dimension named above; an argument that names none is the same for every part. Nothing has to cross between parts.
All inputs are finite; a program needn't handle non-finite values.
Results may differ from the reference program's by a relative error of at most 0.0045.
Values may be sent and summed in bfloat16 or wider, within the bound.
No kernel may reach another device: no remote copies, remote signals or barrier semaphores. Data moves between devices by JAX's collectives and lax.ppermute only.
A program may use at most 128 MiB of HBM per device.

```python
import math
import jax
import jax.numpy as jnp
from jax import lax

D = 1152
HEAD_DIM = 72
HEADS = 8
CH = 16
TEMB = 256
STEPS = 1000
REACH = 2
WC = 32
B = 2
HD = 576
FRAMES = 8
ROWS = 16


def video_sample(key):
    sample = jax.random.normal(key, (B, FRAMES, ROWS, WC, CH), jnp.float32)
    return jnp.clip(sample, -6.0, 6.0)


def drawn_projection(key):
    keys_all = jax.random.split(key, 3)
    spread_factor = D ** (-0.5)
    query_weight = jax.random.normal(keys_all[0], (D, HD), jnp.float32) * spread_factor
    key_weight = jax.random.normal(keys_all[1], (D, HD), jnp.float32) * spread_factor
    value_weight = jax.random.normal(keys_all[2], (D, HD), jnp.float32) * spread_factor
    return jnp.concatenate([query_weight, key_weight, value_weight], axis=1).astype(jnp.bfloat16)


def draw_latents(key, part):
    return video_sample(jax.random.fold_in(key, 11))


def draw_target_noise(key, part):
    return video_sample(jax.random.fold_in(key, 23))


def draw_spatial_project(key, part):
    return drawn_projection(jax.random.fold_in(key, 31))


def draw_temporal_project(key, part):
    return drawn_projection(jax.random.fold_in(key, 47))


def normal_values(own_key, extent, width, bound, kind=jnp.bfloat16):
    return jnp.clip(width * jax.random.normal(own_key, extent, jnp.float32), -bound, bound).astype(kind)


def setup_inputs(seed: int = 0, part: int = 0) -> dict:
    keys = jax.random.split(jax.random.key(seed), 11)
    part_keys = jax.random.split(jax.random.fold_in(keys[10], part), 11)
    latents = draw_latents(jax.random.fold_in(jax.random.fold_in(keys[10], part), 71), part)
    target_noise = draw_target_noise(jax.random.fold_in(jax.random.fold_in(keys[10], part), 71), part)
    timesteps = jax.random.randint(part_keys[2], (B,), 0, STEPS).astype(jnp.int32)
    patch_weight = normal_values(keys[3], (CH, D), CH ** -0.5, 1.5)
    time_weight = normal_values(keys[4], (TEMB, D), (TEMB // 2) ** -0.5, 0.5)
    spatial_project = draw_spatial_project(jax.random.fold_in(keys[10], 71), part)
    spatial_output = normal_values(keys[6], (HD, D), (HD // 9) ** -0.5, 0.75)
    temporal_project = draw_temporal_project(jax.random.fold_in(keys[10], 71), part)
    temporal_output = normal_values(keys[8], (HD, D), (HD // 9) ** -0.5, 0.75)
    final_weight = normal_values(keys[9], (D, CH), D ** -0.5, 0.1875)
    return dict(latents=latents, target_noise=target_noise, timesteps=timesteps, patch_weight=patch_weight, time_weight=time_weight, spatial_project=spatial_project, spatial_output=spatial_output, temporal_project=temporal_project, temporal_output=temporal_output, final_weight=final_weight)


def to_wide(array):
    return lax.optimization_barrier(array).astype(jnp.float32)

def layer_norm(stream):
    average = lax.optimization_barrier(jnp.mean(stream, axis=-1, keepdims=True))
    centred = stream - average
    variance = lax.optimization_barrier(jnp.mean(centred * centred, axis=-1, keepdims=True))
    return centred * lax.rsqrt(variance + 1e-06)

def noise_levels(timesteps):
    counter = jnp.arange(STEPS, dtype=jnp.float32)
    betas_all = 0.0001 + (0.02 - 0.0001) * counter / (STEPS - 1)
    log_keep = jnp.cumsum(jnp.log1p(-betas_all))
    selector = (jnp.arange(STEPS, dtype=jnp.int32)[None, :] == timesteps.astype(jnp.int32)[:, None]).astype(jnp.float32)
    log_bar = jnp.dot(selector, log_keep, precision=lax.Precision.HIGHEST)
    kept_share = jnp.exp(log_bar)
    return (jnp.sqrt(kept_share), jnp.sqrt(1.0 - kept_share))

def time_embed(timesteps, time_weight):
    halfway = time_weight.shape[0] // 2
    freqs_all = jnp.exp(-math.log(10000.0) * jnp.arange(halfway, dtype=jnp.float32) / halfway)
    angles = timesteps.astype(jnp.float32)[:, None] * freqs_all[None, :]
    features = jnp.concatenate([jnp.cos(angles), jnp.sin(angles)], axis=-1).astype(jnp.bfloat16)
    return jnp.dot(features, time_weight, preferred_element_type=jnp.float32)

def softmax_rows(scores):
    row_top = lax.optimization_barrier(jnp.max(scores, axis=-1, keepdims=True))
    exponent = jnp.exp(scores - row_top)
    return (exponent / lax.optimization_barrier(jnp.sum(exponent, axis=-1, keepdims=True))).astype(jnp.bfloat16)

def spatial_attend(queries, padded, first_row, total_rows):
    batches, frames_n, rows_n, cols_n, inner_width = queries.shape
    window_rows = 2 * REACH + 1
    windows = jnp.concatenate([padded[:, :, offset:offset + rows_n] for offset in range(window_rows)], axis=3)
    heads_query = queries.reshape(batches, frames_n, rows_n, cols_n, HEADS, HEAD_DIM)
    key_part = windows[..., :inner_width].reshape(batches, frames_n, rows_n, window_rows * cols_n, HEADS, HEAD_DIM)
    value_part = windows[..., inner_width:].reshape(batches, frames_n, rows_n, window_rows * cols_n, HEADS, HEAD_DIM)
    scores = jnp.einsum('bfrqhe,bfrkhe->bfrhqk', to_wide(heads_query), to_wide(key_part), precision=lax.Precision.HIGHEST) / math.sqrt(HEAD_DIM)
    key_rows = first_row + jnp.arange(rows_n, dtype=jnp.int32)[:, None] + jnp.arange(window_rows * cols_n, dtype=jnp.int32)[None, :] // cols_n - REACH
    inside = (key_rows >= 0) & (key_rows < total_rows)
    scores = jnp.where(inside[None, None, :, None, None, :], scores, -1e+30)
    weights = softmax_rows(scores)
    mixed_out = jnp.einsum('bfrhqk,bfrkhe->bfrqhe', to_wide(weights), to_wide(value_part), precision=lax.Precision.HIGHEST)
    return mixed_out.astype(jnp.bfloat16).reshape(batches, frames_n, rows_n, cols_n, inner_width)

def temporal_attend(projected):
    batches, frames_n, places, triple = projected.shape
    inner_width = triple // 3
    shaped = projected.reshape(batches, frames_n, places, 3, HEADS, HEAD_DIM)
    scores = jnp.einsum('bfphe,bgphe->bphfg', to_wide(shaped[:, :, :, 0]), to_wide(shaped[:, :, :, 1]), precision=lax.Precision.HIGHEST) / math.sqrt(HEAD_DIM)
    weights = softmax_rows(scores)
    mixed_out = jnp.einsum('bphfg,bgphe->bfphe', to_wide(weights), to_wide(shaped[:, :, :, 2]), precision=lax.Precision.HIGHEST)
    return mixed_out.astype(jnp.bfloat16).reshape(batches, frames_n, places, inner_width)

def reference(latents, target_noise, timesteps, patch_weight, time_weight, spatial_project, spatial_output, temporal_project, temporal_output, final_weight):
    signal, spread = noise_levels(timesteps)
    noisy_input = (signal[:, None, None, None, None] * latents + spread[:, None, None, None, None] * target_noise).astype(jnp.bfloat16)
    time_vector = time_embed(timesteps, time_weight)
    stream = jnp.dot(noisy_input, patch_weight, preferred_element_type=jnp.float32) + time_vector[:, None, None, None, :]
    batches, frames_n, rows_n, cols_n, model_width = stream.shape
    inner_width = spatial_output.shape[0]
    normed = layer_norm(stream).astype(jnp.bfloat16)
    projected = jnp.dot(normed, spatial_project, preferred_element_type=jnp.float32).astype(jnp.bfloat16)
    padded = jnp.pad(projected[..., inner_width:], ((0, 0), (0, 0), (REACH, REACH), (0, 0), (0, 0)))
    mixed_out = spatial_attend(projected[..., :inner_width], padded, 0, ROWS)
    stream = stream + jnp.dot(mixed_out, spatial_output, preferred_element_type=jnp.float32)
    normed = layer_norm(stream).astype(jnp.bfloat16).reshape(batches, frames_n, rows_n * cols_n, model_width)
    projected = jnp.dot(normed, temporal_project, preferred_element_type=jnp.float32).astype(jnp.bfloat16)
    mixed_out = temporal_attend(projected)
    temporal_delta = jnp.dot(mixed_out, temporal_output, preferred_element_type=jnp.float32)
    stream = stream + temporal_delta.reshape(stream.shape)
    normed = layer_norm(stream).astype(jnp.bfloat16)
    predicted = jnp.dot(normed, final_weight, preferred_element_type=jnp.float32)
    residual_gap = predicted - target_noise
    return lax.optimization_barrier(jnp.mean(residual_gap * residual_gap, axis=-1))
```

```python
import functools
import math

import jax
import jax.numpy as jnp
from jax import lax
from jax.experimental import pallas as pl
from jax.experimental.pallas import tpu as pltpu
from jax.sharding import PartitionSpec as P

HEAD_DIM = 72
HEADS = 8
STEPS = 1000
REACH = 2
EPS = 1e-06
LANES = 128
BASIS = 24
VPAD = 80
F32 = jnp.float32
BF16 = jnp.bfloat16
VMEM = pl.BlockSpec(memory_space=pltpu.VMEM)
SMEM = pl.BlockSpec(memory_space=pltpu.SMEM)


def dot(a, b, ca=1, cb=0, precision=None):
    return lax.dot_general(
        a, b, (((ca,), (cb,)), ((), ())), preferred_element_type=F32, precision=precision
    )


def split(x):
    high = x.astype(BF16).astype(F32)
    return high, x - high


def iota(shape, dim):
    return lax.broadcasted_iota(jnp.int32, shape, dim)


def cat(parts, axis):
    return parts[0] if len(parts) == 1 else jnp.concatenate(parts, axis=axis)


class Plan:
    def __init__(self, videos, rows, cols, frames, halves):
        self.videos, self.rows, self.cols = videos, rows, cols
        self.frames, self.halves = frames, halves
        self.chunks = frames // videos
        self.places = rows * cols // self.chunks
        self.qrows = max(1, self.places // cols)
        self.window = (self.qrows + 2 * REACH) * cols
        self.width = -(-(self.window + 3 * self.places) // LANES) * LANES
        self.tokens = frames * self.places
        self.low = LANES // frames
        whole = self.qrows * cols if self.places >= cols else cols
        assert frames % videos == 0 and (rows * cols) % self.chunks == 0
        assert self.places % cols == 0 or cols % self.places == 0
        assert rows >= REACH and rows % self.qrows == 0 and whole >= self.places
        for size in (cols, frames, self.places, self.low):
            assert size & (size - 1) == 0 and size > 0
        assert self.places % self.low == 0 and self.tokens % LANES == 0


def log_kept(step):
    counter = iota((8, LANES), 0) * LANES + iota((8, LANES), 1)
    beta = 0.0001 + (0.02 - 0.0001) * counter.astype(F32) / (STEPS - 1)
    used = (counter <= step) & (counter < STEPS)
    terms = jnp.where(used, jnp.log1p(-jnp.where(used, beta, 0.0)), 0.0)
    return jnp.sum(jnp.sum(terms, axis=0, keepdims=True), axis=1, keepdims=True)


def pack_kernel(plan, steps_ref, latents_ref, noise_ref, send_ref):
    half = lax.axis_index("row")
    channels = latents_ref.shape[1]
    size = plan.rows * plan.cols
    eye = (iota((channels, channels), 0) == iota((channels, channels), 1)).astype(BF16)
    videos = []
    for video in range(plan.videos):
        kept = jnp.exp(log_kept(steps_ref[video]))
        signal, spread = jnp.sqrt(kept), jnp.sqrt(1.0 - kept)
        rows = pl.ds(video * size, size)
        noise = noise_ref[rows, :]
        noisy = (signal * latents_ref[rows, :] + spread * noise).astype(BF16)
        high, rest = split(noise)
        videos.append(
            [dot(eye, part, 1, 1) for part in (noisy, high.astype(BF16), rest.astype(BF16))]
        )

    def window(value, start, count):
        first, last = max(start, 0), min(start + count, plan.rows)
        if first >= last:
            return jnp.zeros((channels, count * plan.cols), F32)
        parts = []
        if first > start:
            parts.append(jnp.zeros((channels, (first - start) * plan.cols), F32))
        parts.append(value[:, first * plan.cols : last * plan.cols])
        if last < start + count:
            parts.append(jnp.zeros((channels, (start + count - last) * plan.cols), F32))
        return cat(parts, 1)

    unused = plan.width - plan.window - 3 * plan.places
    for target in range(plan.halves):
        for apart in range(1 - plan.halves, plan.halves):
            if not 0 <= target + apart < plan.halves:
                continue

            @pl.when(half == target + apart)
            def _():
                for peer in range(plan.frames):
                    values = videos[peer // plan.chunks]
                    place = (peer % plan.chunks) * plan.places
                    start = place // plan.cols - REACH - apart * plan.rows
                    parts = [window(values[0], start, plan.qrows + 2 * REACH)]
                    if apart == 0:
                        parts += [v[:, place : place + plan.places] for v in values]
                        if unused:
                            parts.append(jnp.zeros((channels, unused), F32))
                    else:
                        parts.append(jnp.zeros((channels, plan.width - plan.window), F32))
                    send_ref[peer * plan.halves + target] = cat(parts, 1).astype(BF16)


def fold_kernel(
    plan,
    steps_ref,
    patch_ref,
    time_ref,
    sproject_ref,
    soutput_ref,
    tproject_ref,
    toutput_ref,
    final_ref,
    gram_ref,
    score_ref,
    mixt_ref,
    query_ref,
    key_ref,
    value_ref,
    outt_ref,
    finalt_ref,
):
    model = patch_ref.shape[1]
    inner = soutput_ref.shape[0]
    channels = patch_ref.shape[0]
    halfway = time_ref.shape[0] // 2
    scale = math.log2(math.e) / math.sqrt(HEAD_DIM)
    step = steps_ref[lax.axis_index("frame") // plan.chunks]

    freqs = jnp.exp(iota((8, halfway), 1).astype(F32) * (-math.log(10000.0) / halfway))
    angles = step.astype(F32) * freqs
    features = jnp.concatenate([jnp.cos(angles), jnp.sin(angles)], axis=1).astype(BF16)
    time_vector = dot(features, time_ref[...])
    time_rows = jnp.where(iota((8, model), 0) == 0, time_vector, 0.0)
    basis = jnp.concatenate([patch_ref[...].astype(F32), time_rows], axis=0)
    basis = basis - jnp.mean(basis, axis=1, keepdims=True)

    gram = dot(basis, basis, 1, 1, lax.Precision.HIGHEST) * (1.0 / model)
    high, rest = split(gram)
    middle, low = split(rest)
    gram_ref[...] = jnp.concatenate([high, middle, low], axis=0).astype(BF16)

    high, rest = split(basis)
    both = dot(jnp.concatenate([high, rest], axis=0).astype(BF16), sproject_ref[...])
    folded = both[:BASIS] + both[BASIS:]
    queries, keys, values = (folded[:, i * inner : (i + 1) * inner] for i in range(3))
    lane = iota((BASIS, inner), 1)

    def by_head(value):
        return jnp.concatenate(
            [
                jnp.where((lane >= h * HEAD_DIM) & (lane < (h + 1) * HEAD_DIM), value, 0.0)
                for h in range(HEADS)
            ],
            axis=0,
        )

    score_ref[...] = dot(by_head(keys), queries * scale, 1, 1, lax.Precision.HIGHEST)

    high, rest = split(by_head(values))
    both = dot(jnp.concatenate([high, rest], axis=0).astype(BF16), soutput_ref[...])
    mixed = both[: HEADS * BASIS] + both[HEADS * BASIS :]
    mixed = mixed - jnp.mean(mixed, axis=1, keepdims=True)
    depth = mixt_ref.shape[1]
    unused = depth - (HEADS + 1) * BASIS
    whole = jnp.concatenate([basis, mixed, jnp.zeros((unused, model), F32)], axis=0)
    mixt_ref[...] = whole.T.astype(BF16)

    folded = dot(whole.astype(BF16), tproject_ref[...])
    queries = (folded[:, :inner] * scale).T
    keys = folded[:, inner : 2 * inner]
    values = folded[:, 2 * inner :].T
    for h in range(HEADS):
        cut = slice(h * HEAD_DIM, (h + 1) * HEAD_DIM)
        query_ref[pl.ds(h * LANES, LANES), :] = jnp.concatenate(
            [queries[cut], jnp.zeros((LANES - HEAD_DIM, depth), F32)], axis=0
        ).astype(BF16)
        key_ref[:, pl.ds(h * LANES, LANES)] = jnp.concatenate(
            [keys[:, cut], jnp.zeros((depth, LANES - HEAD_DIM), F32)], axis=1
        ).astype(BF16)
        value_ref[pl.ds(h * VPAD, VPAD), :] = jnp.concatenate(
            [values[cut], jnp.zeros((VPAD - HEAD_DIM, depth), F32)], axis=0
        ).astype(BF16)

    outt_ref[...] = toutput_ref[...].T
    eye = (iota((channels, channels), 0) == iota((channels, channels), 1)).astype(BF16)
    finalt_ref[...] = dot(eye, final_ref[...], 1, 1).astype(BF16)


def main_kernel(
    plan,
    recv_ref,
    gram_ref,
    score_ref,
    mixt_ref,
    query_ref,
    key_ref,
    value_ref,
    outt_ref,
    finalt_ref,
    out_ref,
    mixed_ref,
    stream_ref,
):
    window, places, tokens = plan.window, plan.places, plan.tokens
    channels = recv_ref.shape[1]
    depth = mixt_ref.shape[1]
    spread = HEADS * places
    half = lax.axis_index("row")
    chunk = lax.rem(lax.axis_index("frame"), plan.chunks)
    top = half * plan.rows + lax.div(chunk * places, plan.cols) - REACH

    def with_one(value):
        one = (iota((BASIS - channels, value.shape[1]), 0) == 0).astype(F32)
        return jnp.concatenate([value, one], axis=0)

    gram = gram_ref[...]

    def normalised(value):
        parts = dot(gram, value.astype(BF16))
        image = parts[:BASIS] + parts[BASIS : 2 * BASIS] + parts[2 * BASIS :]
        variance = jnp.sum(value * image, axis=0, keepdims=True)
        return value * lax.rsqrt(jnp.maximum(variance, 0.0) + EPS)

    received = []
    for f in range(plan.frames):
        value = recv_ref[f * plan.halves].astype(F32)
        for r in range(1, plan.halves):
            value = value + recv_ref[f * plan.halves + r].astype(F32)
        received.append(value)
    own, noise_high, noise_rest = (
        cat([v[:, window + i * places : window + (i + 1) * places] for v in received], 1)
        for i in range(3)
    )
    own = with_one(own)
    high, rest = split(normalised(own))
    shigh, srest = split(score_ref[...])
    high, shigh = high.astype(BF16), shigh.astype(BF16)
    turned = (
        dot(shigh, high) + dot(shigh, rest.astype(BF16)) + dot(srest.astype(BF16), high)
    )

    key_row = jnp.zeros((window, spread), jnp.int32)
    key_index = iota((window, spread), 0)
    for j in range(1, window // plan.cols):
        key_row = key_row + (key_index >= j * plan.cols).astype(jnp.int32)
    query_row = jnp.zeros((window, spread), jnp.int32)
    query_index = iota((window, spread), 1) & (places - 1)
    for j in range(1, plan.qrows):
        query_row = query_row + (query_index >= j * plan.cols).astype(jnp.int32)
    seen = (key_row >= query_row) & (key_row <= query_row + 2 * REACH)
    seen = seen & (key_row + top >= 0) & (key_row + top < plan.halves * plan.rows)
    mask = jnp.where(seen, 0.0, -1e30)

    gathered = []
    for f in range(plan.frames):
        high, rest = split(normalised(with_one(received[f][:, :window])))
        qhigh, qrest = split(
            cat(
                [
                    turned[h * BASIS : (h + 1) * BASIS, f * places : (f + 1) * places]
                    for h in range(HEADS)
                ],
                1,
            )
        )
        left = jnp.concatenate([high, high, rest], axis=0).astype(BF16)
        right = jnp.concatenate([qhigh, qrest, qhigh], axis=0).astype(BF16)
        scores = dot(left, right, 0, 0) + mask
        weights = jnp.exp2(scores - jnp.max(scores, axis=0, keepdims=True)).astype(BF16)
        ones = (iota((8, window), 0) == 0).astype(F32)
        left = jnp.concatenate([high, rest, ones], axis=0).astype(BF16)
        sums = dot(left, weights)
        mean = (sums[:BASIS] + sums[BASIS : 2 * BASIS]) / sums[2 * BASIS : 2 * BASIS + 1]
        gathered.append(
            jnp.concatenate(
                [mean[:, h * places : (h + 1) * places] for h in range(HEADS)], axis=0
            )
        )
    unused = depth - (HEADS + 1) * BASIS
    combined = jnp.concatenate(
        [own, cat(gathered, 1), jnp.zeros((unused, tokens), F32)], axis=0
    )

    def source(shape, dim):
        m = iota(shape, dim)
        group, frame, low = m // LANES, (m & (LANES - 1)) // plan.low, m & (plan.low - 1)
        return frame * places + group * plan.low + low

    order = (iota((tokens, tokens), 0) == source((tokens, tokens), 1)).astype(BF16)
    back = (iota((tokens, tokens), 1) == source((tokens, tokens), 0)).astype(BF16)
    high, rest = split(combined)
    combined = dot(high.astype(BF16), order) + dot(rest.astype(BF16), order)
    noise = dot(noise_high.astype(BF16), order) + dot(noise_rest.astype(BF16), order)

    stream = dot(mixt_ref[...], combined.astype(BF16))
    stream_ref[...] = stream
    variance = jnp.mean(stream * stream, axis=0, keepdims=True)
    combined = (combined * lax.rsqrt(variance + EPS)).astype(BF16)
    queries = dot(query_ref[...], combined).astype(BF16)
    keys = dot(combined, key_ref[...], 0, 0).astype(BF16)
    values = dot(value_ref[...], combined).astype(BF16)
    same = (iota((LANES, LANES), 0) & (plan.low - 1)) == (
        iota((LANES, LANES), 1) & (plan.low - 1)
    )
    mask = jnp.where(same, 0.0, -1e30)
    for g in range(tokens // LANES):
        cut = slice(g * LANES, (g + 1) * LANES)
        for h in range(HEADS):
            head = slice(h * LANES, (h + 1) * LANES)
            scores = dot(keys[cut, head], queries[head, cut]) + mask
            weights = jnp.exp2(scores - jnp.max(scores, axis=0, keepdims=True))
            total = jnp.sum(weights, axis=0, keepdims=True)
            mean = dot(values[h * VPAD : (h + 1) * VPAD, cut], weights.astype(BF16)) / total
            mixed_ref[pl.ds(h * HEAD_DIM, HEAD_DIM), pl.ds(g * LANES, LANES)] = mean[:HEAD_DIM]

    stream = stream_ref[...] + dot(outt_ref[...], mixed_ref[...].astype(BF16))
    stream = stream - jnp.mean(stream, axis=0, keepdims=True)
    variance = jnp.mean(stream * stream, axis=0, keepdims=True)
    normed = (stream * lax.rsqrt(variance + EPS)).astype(BF16)
    gap = dot(finalt_ref[...], normed) - noise
    errors = jnp.mean(gap * gap, axis=0, keepdims=True)
    high, rest = split(errors)
    middle, low = split(rest)
    parts = jnp.concatenate([high, middle, low] + [jnp.zeros_like(low)] * 5, axis=0)
    errors = jnp.sum(dot(parts.astype(BF16), back), axis=0, keepdims=True)
    for f in range(plan.frames):
        out_ref[pl.ds(f, 1), :] = errors[:, f * places : (f + 1) * places]


def local(
    latents,
    target_noise,
    timesteps,
    patch_weight,
    time_weight,
    spatial_project,
    spatial_output,
    temporal_project,
    temporal_output,
    final_weight,
):
    videos, _, rows, cols, channels = latents.shape
    frames, halves = lax.axis_size("frame"), lax.axis_size("row")
    plan = Plan(videos, rows, cols, frames, halves)
    inner, model = spatial_output.shape
    depth = -(-(HEADS + 1) * BASIS // LANES) * LANES
    shape = jax.ShapeDtypeStruct

    send = pl.pallas_call(
        functools.partial(pack_kernel, plan),
        out_shape=shape((frames * halves, channels, plan.width), BF16),
        in_specs=[SMEM, VMEM, VMEM],
        out_specs=VMEM,
    )(timesteps, latents.reshape(-1, channels), target_noise.reshape(-1, channels))
    received = lax.all_to_all(send, ("frame", "row"), 0, 0, tiled=True)

    tables = pl.pallas_call(
        functools.partial(fold_kernel, plan),
        out_shape=(
            shape((3 * BASIS, BASIS), BF16),
            shape((HEADS * BASIS, BASIS), F32),
            shape((model, depth), BF16),
            shape((HEADS * LANES, depth), BF16),
            shape((depth, HEADS * LANES), BF16),
            shape((HEADS * VPAD, depth), BF16),
            shape((model, inner), BF16),
            shape((channels, model), BF16),
        ),
        in_specs=[SMEM] + [VMEM] * 7,
        out_specs=(VMEM,) * 8,
    )(
        timesteps,
        patch_weight,
        time_weight,
        spatial_project,
        spatial_output,
        temporal_project,
        temporal_output,
        final_weight,
    )

    errors = pl.pallas_call(
        functools.partial(main_kernel, plan),
        out_shape=shape((frames, plan.places), F32),
        in_specs=[VMEM] * 9,
        out_specs=VMEM,
        scratch_shapes=[
            pltpu.VMEM((inner, plan.tokens), F32),
            pltpu.VMEM((model, plan.tokens), F32),
        ],
    )(received, *tables)
    errors = lax.all_to_all(errors, "frame", 0, 0, tiled=True)
    return errors.reshape(videos, 1, rows, cols)


def solution(mesh):
    return jax.shard_map(
        local,
        mesh=mesh,
        in_specs=(
            P("grp", "frame", "row", None, None),
            P("grp", "frame", "row", None, None),
            P("grp"),
            P(),
            P(),
            P(),
            P(),
            P(),
            P(),
            P(),
        ),
        out_specs=P("grp", "frame", "row", None),
        check_vma=False,
    )
```

```python
import functools
import math

import jax
import jax.numpy as jnp
from jax import lax
from jax.experimental import pallas as pl
from jax.experimental.pallas import tpu as pltpu
from jax.sharding import PartitionSpec as P

HEAD_DIM = 72
HEADS = 8
STEPS = 1000
REACH = 2
EPS = 1e-06
LANES = 128
BASIS = 24
VPAD = 80
F32 = jnp.float32
BF16 = jnp.bfloat16
VMEM = pl.BlockSpec(memory_space=pltpu.VMEM)
SMEM = pl.BlockSpec(memory_space=pltpu.SMEM)


def dot(a, b, ca=1, cb=0, precision=None):
    return lax.dot_general(
        a, b, (((ca,), (cb,)), ((), ())), preferred_element_type=F32, precision=precision
    )


def split(x):
    high = x.astype(BF16).astype(F32)
    return high, x - high


def iota(shape, dim):
    return lax.broadcasted_iota(jnp.int32, shape, dim)


def cat(parts, axis):
    return parts[0] if len(parts) == 1 else jnp.concatenate(parts, axis=axis)


class Plan:
    def __init__(self, videos, rows, cols, frames, halves):
        self.videos, self.rows, self.cols = videos, rows, cols
        self.frames, self.halves = frames, halves
        self.chunks = frames // videos
        self.places = rows * cols // self.chunks
        self.qrows = max(1, self.places // cols)
        self.window = (self.qrows + 2 * REACH) * cols
        self.width = -(-(self.window + 3 * self.places) // LANES) * LANES
        self.tokens = frames * self.places
        self.low = LANES // frames
        whole = self.qrows * cols if self.places >= cols else cols
        assert frames % videos == 0 and (rows * cols) % self.chunks == 0
        assert self.places % cols == 0 or cols % self.places == 0
        assert rows >= REACH and rows % self.qrows == 0 and whole >= self.places
        for size in (cols, frames, self.places, self.low):
            assert size & (size - 1) == 0 and size > 0
        assert self.places % self.low == 0 and self.tokens % LANES == 0


def log_kept(step):
    counter = iota((8, LANES), 0) * LANES + iota((8, LANES), 1)
    beta = 0.0001 + (0.02 - 0.0001) * counter.astype(F32) / (STEPS - 1)
    used = (counter <= step) & (counter < STEPS)
    terms = jnp.where(used, jnp.log1p(-jnp.where(used, beta, 0.0)), 0.0)
    return jnp.sum(jnp.sum(terms, axis=0, keepdims=True), axis=1, keepdims=True)


def pack_kernel(plan, steps_ref, latents_ref, noise_ref, send_ref):
    half = lax.axis_index("row")
    channels = latents_ref.shape[2]
    videos = []
    for video in range(plan.videos):
        kept = jnp.exp(log_kept(steps_ref[video]))
        signal, spread = jnp.sqrt(kept), jnp.sqrt(1.0 - kept)
        noise = cat([noise_ref[video, row] for row in range(plan.rows)], 1)
        clean = cat([latents_ref[video, row] for row in range(plan.rows)], 1)
        videos.append((signal * clean + spread * noise, *split(noise)))

    def window(value, start, count):
        first, last = max(start, 0), min(start + count, plan.rows)
        if first >= last:
            return jnp.zeros((channels, count * plan.cols), F32)
        parts = []
        if first > start:
            parts.append(jnp.zeros((channels, (first - start) * plan.cols), F32))
        parts.append(value[:, first * plan.cols : last * plan.cols])
        if last < start + count:
            parts.append(jnp.zeros((channels, (start + count - last) * plan.cols), F32))
        return cat(parts, 1)

    unused = plan.width - plan.window - 3 * plan.places
    for target in range(plan.halves):
        for apart in range(1 - plan.halves, plan.halves):
            if not 0 <= target + apart < plan.halves:
                continue

            @pl.when(half == target + apart)
            def _():
                for peer in range(plan.frames):
                    values = videos[peer // plan.chunks]
                    place = (peer % plan.chunks) * plan.places
                    start = place // plan.cols - REACH - apart * plan.rows
                    parts = [window(values[0], start, plan.qrows + 2 * REACH)]
                    if apart == 0:
                        parts += [v[:, place : place + plan.places] for v in values]
                        if unused:
                            parts.append(jnp.zeros((channels, unused), F32))
                    else:
                        parts.append(jnp.zeros((channels, plan.width - plan.window), F32))
                    send_ref[peer * plan.halves + target] = cat(parts, 1).astype(BF16)


def fold_kernel(
    plan,
    steps_ref,
    patch_ref,
    time_ref,
    sproject_ref,
    soutput_ref,
    tproject_ref,
    toutput_ref,
    gram_ref,
    score_ref,
    mixt_ref,
    query_ref,
    key_ref,
    value_ref,
    outt_ref,
):
    model = patch_ref.shape[1]
    inner = soutput_ref.shape[0]
    channels = patch_ref.shape[0]
    halfway = time_ref.shape[0] // 2
    scale = math.log2(math.e) / math.sqrt(HEAD_DIM)
    step = steps_ref[lax.axis_index("frame") // plan.chunks]

    freqs = jnp.exp(iota((8, halfway), 1).astype(F32) * (-math.log(10000.0) / halfway))
    angles = step.astype(F32) * freqs
    features = jnp.concatenate([jnp.cos(angles), jnp.sin(angles)], axis=1).astype(BF16)
    time_vector = dot(features, time_ref[...])
    time_rows = jnp.where(iota((8, model), 0) == 0, time_vector, 0.0)
    basis = jnp.concatenate([patch_ref[...].astype(F32), time_rows], axis=0)
    basis = basis - jnp.mean(basis, axis=1, keepdims=True)

    gram = dot(basis, basis, 1, 1, lax.Precision.HIGHEST) * (1.0 / model)
    high, rest = split(gram)
    middle, low = split(rest)
    gram_ref[...] = jnp.concatenate([high, middle, low], axis=0).astype(BF16)

    high, rest = split(basis)
    both = dot(jnp.concatenate([high, rest], axis=0).astype(BF16), sproject_ref[...], 1, 1)
    folded = both[:BASIS] + both[BASIS:]
    queries, keys, values = (folded[:, i * inner : (i + 1) * inner] for i in range(3))
    lane = iota((BASIS, inner), 1)

    def by_head(value):
        return jnp.concatenate(
            [
                jnp.where((lane >= h * HEAD_DIM) & (lane < (h + 1) * HEAD_DIM), value, 0.0)
                for h in range(HEADS)
            ],
            axis=0,
        )

    score_ref[...] = dot(by_head(keys), queries * scale, 1, 1, lax.Precision.HIGHEST)

    high, rest = split(by_head(values))
    both = dot(jnp.concatenate([high, rest], axis=0).astype(BF16), soutput_ref[...])
    mixed = both[: HEADS * BASIS] + both[HEADS * BASIS :]
    mixed = mixed - jnp.mean(mixed, axis=1, keepdims=True)
    depth = mixt_ref.shape[1]
    unused = depth - (HEADS + 1) * BASIS
    whole = jnp.concatenate([basis, mixed, jnp.zeros((unused, model), F32)], axis=0)
    mixt_ref[...] = whole.T.astype(BF16)

    folded = dot(tproject_ref[...], whole.astype(BF16), 1, 1)
    keys = []
    for h in range(HEADS):
        query, key, value = (
            folded[i * inner + h * HEAD_DIM : i * inner + (h + 1) * HEAD_DIM] for i in range(3)
        )
        unused = jnp.zeros((LANES - HEAD_DIM, depth), F32)
        keys += [key, unused]
        query_ref[pl.ds(h * LANES, LANES), :] = jnp.concatenate(
            [query * scale, unused], axis=0
        ).astype(BF16)
        value_ref[pl.ds(h * VPAD, VPAD), :] = jnp.concatenate(
            [value, unused[: VPAD - HEAD_DIM]], axis=0
        ).astype(BF16)
    key_ref[...] = jnp.concatenate(keys, axis=0).T.astype(BF16)

    outt_ref[...] = toutput_ref[...].T


def main_kernel(
    plan,
    recv_ref,
    gram_ref,
    score_ref,
    mixt_ref,
    query_ref,
    key_ref,
    value_ref,
    outt_ref,
    finalt_ref,
    out_ref,
    mixed_ref,
    stream_ref,
):
    window, places, tokens = plan.window, plan.places, plan.tokens
    channels = recv_ref.shape[1]
    depth = mixt_ref.shape[1]
    spread = HEADS * places
    half = lax.axis_index("row")
    chunk = lax.rem(lax.axis_index("frame"), plan.chunks)
    top = half * plan.rows + lax.div(chunk * places, plan.cols) - REACH

    def with_one(value):
        one = (iota((BASIS - channels, value.shape[1]), 0) == 0).astype(F32)
        return jnp.concatenate([value, one], axis=0)

    gram = gram_ref[...]

    def normalised(value):
        parts = dot(gram, value.astype(BF16))
        image = parts[:BASIS] + parts[BASIS : 2 * BASIS] + parts[2 * BASIS :]
        variance = jnp.sum(value * image, axis=0, keepdims=True)
        return value * lax.rsqrt(jnp.maximum(variance, 0.0) + EPS)

    received = []
    for f in range(plan.frames):
        value = recv_ref[f * plan.halves].astype(F32)
        for r in range(1, plan.halves):
            value = value + recv_ref[f * plan.halves + r].astype(F32)
        received.append(value)
    own, noise_high, noise_rest = (
        cat([v[:, window + i * places : window + (i + 1) * places] for v in received], 1)
        for i in range(3)
    )
    own = with_one(own)
    high, rest = split(normalised(own))
    shigh, srest = split(score_ref[...])
    high, shigh = high.astype(BF16), shigh.astype(BF16)
    turned = (
        dot(shigh, high) + dot(shigh, rest.astype(BF16)) + dot(srest.astype(BF16), high)
    )

    key_row = jnp.zeros((window, spread), jnp.int32)
    key_index = iota((window, spread), 0)
    for j in range(1, window // plan.cols):
        key_row = key_row + (key_index >= j * plan.cols).astype(jnp.int32)
    query_row = jnp.zeros((window, spread), jnp.int32)
    query_index = iota((window, spread), 1) & (places - 1)
    for j in range(1, plan.qrows):
        query_row = query_row + (query_index >= j * plan.cols).astype(jnp.int32)
    seen = (key_row >= query_row) & (key_row <= query_row + 2 * REACH)
    seen = seen & (key_row + top >= 0) & (key_row + top < plan.halves * plan.rows)
    mask = jnp.where(seen, 0.0, -1e30)

    gathered = []
    for f in range(plan.frames):
        high, rest = split(normalised(with_one(received[f][:, :window])))
        qhigh, qrest = split(
            cat(
                [
                    turned[h * BASIS : (h + 1) * BASIS, f * places : (f + 1) * places]
                    for h in range(HEADS)
                ],
                1,
            )
        )
        left = jnp.concatenate([high, high, rest], axis=0).astype(BF16)
        right = jnp.concatenate([qhigh, qrest, qhigh], axis=0).astype(BF16)
        scores = dot(left, right, 0, 0) + mask
        weights = jnp.exp2(scores - jnp.max(scores, axis=0, keepdims=True)).astype(BF16)
        ones = (iota((8, window), 0) == 0).astype(F32)
        left = jnp.concatenate([high, rest, ones], axis=0).astype(BF16)
        sums = dot(left, weights)
        mean = (sums[:BASIS] + sums[BASIS : 2 * BASIS]) / sums[2 * BASIS : 2 * BASIS + 1]
        gathered.append(
            jnp.concatenate(
                [mean[:, h * places : (h + 1) * places] for h in range(HEADS)], axis=0
            )
        )
    unused = depth - (HEADS + 1) * BASIS
    combined = jnp.concatenate(
        [own, cat(gathered, 1), jnp.zeros((unused, tokens), F32)], axis=0
    )

    def source(shape, dim):
        m = iota(shape, dim)
        group, frame, low = m // LANES, (m & (LANES - 1)) // plan.low, m & (plan.low - 1)
        return frame * places + group * plan.low + low

    order = (iota((tokens, tokens), 0) == source((tokens, tokens), 1)).astype(BF16)
    back = (iota((tokens, tokens), 1) == source((tokens, tokens), 0)).astype(BF16)
    high, rest = split(combined)
    combined = dot(high.astype(BF16), order) + dot(rest.astype(BF16), order)
    noise = dot(noise_high.astype(BF16), order) + dot(noise_rest.astype(BF16), order)

    stream = dot(mixt_ref[...], combined.astype(BF16))
    stream_ref[...] = stream
    variance = jnp.mean(stream * stream, axis=0, keepdims=True)
    combined = (combined * lax.rsqrt(variance + EPS)).astype(BF16)
    queries = dot(query_ref[...], combined).astype(BF16)
    keys = dot(combined, key_ref[...], 0, 0).astype(BF16)
    values = dot(value_ref[...], combined).astype(BF16)
    same = (iota((LANES, LANES), 0) & (plan.low - 1)) == (
        iota((LANES, LANES), 1) & (plan.low - 1)
    )
    mask = jnp.where(same, 0.0, -1e30)
    for g in range(tokens // LANES):
        cut = slice(g * LANES, (g + 1) * LANES)
        for h in range(HEADS):
            head = slice(h * LANES, (h + 1) * LANES)
            scores = dot(keys[cut, head], queries[head, cut]) + mask
            weights = jnp.exp2(scores - jnp.max(scores, axis=0, keepdims=True))
            total = jnp.sum(weights, axis=0, keepdims=True)
            mean = dot(values[h * VPAD : (h + 1) * VPAD, cut], weights.astype(BF16)) / total
            mixed_ref[pl.ds(h * HEAD_DIM, HEAD_DIM), pl.ds(g * LANES, LANES)] = mean[:HEAD_DIM]

    stream = stream_ref[...] + dot(outt_ref[...], mixed_ref[...].astype(BF16))
    stream = stream - jnp.mean(stream, axis=0, keepdims=True)
    variance = jnp.mean(stream * stream, axis=0, keepdims=True)
    normed = (stream * lax.rsqrt(variance + EPS)).astype(BF16)
    gap = dot(finalt_ref[...], normed) - noise
    errors = jnp.mean(gap * gap, axis=0, keepdims=True)
    high, rest = split(errors)
    middle, low = split(rest)
    parts = jnp.concatenate([high, middle, low] + [jnp.zeros_like(low)] * 5, axis=0)
    errors = jnp.sum(dot(parts.astype(BF16), back), axis=0, keepdims=True)
    lanes = out_ref.shape[1]
    for i in range(tokens // lanes):
        out_ref[pl.ds(i, 1), :] = errors[:, i * lanes : (i + 1) * lanes]


def local(
    latents,
    target_noise,
    timesteps,
    patch_weight,
    time_weight,
    spatial_project,
    spatial_output,
    temporal_project,
    temporal_output,
    final_weight,
):
    videos, _, rows, cols, channels = latents.shape
    frames, halves = lax.axis_size("frame"), lax.axis_size("row")
    plan = Plan(videos, rows, cols, frames, halves)
    inner, model = spatial_output.shape
    depth = -(-(HEADS + 1) * BASIS // LANES) * LANES
    shape = jax.ShapeDtypeStruct

    def by_row(value):
        return value.reshape(videos, rows, cols, channels).transpose(0, 1, 3, 2)

    send = pl.pallas_call(
        functools.partial(pack_kernel, plan),
        out_shape=shape((frames * halves, channels, plan.width), BF16),
        in_specs=[SMEM, VMEM, VMEM],
        out_specs=VMEM,
    )(timesteps, by_row(latents), by_row(target_noise))
    received = lax.all_to_all(send, ("frame", "row"), 0, 0, tiled=True)

    tables = pl.pallas_call(
        functools.partial(fold_kernel, plan),
        out_shape=(
            shape((3 * BASIS, BASIS), BF16),
            shape((HEADS * BASIS, BASIS), F32),
            shape((model, depth), BF16),
            shape((HEADS * LANES, depth), BF16),
            shape((depth, HEADS * LANES), BF16),
            shape((HEADS * VPAD, depth), BF16),
            shape((model, inner), BF16),
        ),
        in_specs=[SMEM] + [VMEM] * 6,
        out_specs=(VMEM,) * 7,
    )(
        timesteps,
        patch_weight,
        time_weight,
        spatial_project.T,
        spatial_output,
        temporal_project.T,
        temporal_output,
    )

    lanes = min(plan.places, cols)
    errors = pl.pallas_call(
        functools.partial(main_kernel, plan),
        out_shape=shape((plan.tokens // lanes, lanes), F32),
        in_specs=[VMEM] * 9,
        out_specs=VMEM,
        scratch_shapes=[
            pltpu.VMEM((inner, plan.tokens), F32),
            pltpu.VMEM((model, plan.tokens), F32),
        ],
    )(received, *tables, final_weight.T)
    errors = lax.all_to_all(errors, "frame", 0, 0, tiled=True)
    return errors.reshape(videos, 1, rows, cols)


def solution(mesh):
    return jax.shard_map(
        local,
        mesh=mesh,
        in_specs=(
            P("grp", "frame", "row", None, None),
            P("grp", "frame", "row", None, None),
            P("grp"),
            P(),
            P(),
            P(),
            P(),
            P(),
            P(),
            P(),
        ),
        out_specs=P("grp", "frame", "row", None),
        check_vma=False,
    )
```

```python
import functools
import math

import jax
import jax.numpy as jnp
from jax import lax
from jax.experimental import pallas as pl
from jax.experimental.pallas import tpu as pltpu
from jax.sharding import PartitionSpec as P

HEAD_DIM = 72
HEADS = 8
STEPS = 1000
REACH = 2
EPS = 1e-06
LANES = 128
BASIS = 24
VPAD = 80
F32 = jnp.float32
BF16 = jnp.bfloat16
VMEM = pl.BlockSpec(memory_space=pltpu.VMEM)
SMEM = pl.BlockSpec(memory_space=pltpu.SMEM)
HBM = pl.BlockSpec(memory_space=pltpu.HBM)


def dot(a, b, ca=1, cb=0, precision=None):
    return lax.dot_general(
        a, b, (((ca,), (cb,)), ((), ())), preferred_element_type=F32, precision=precision
    )


def split(x):
    high = x.astype(BF16).astype(F32)
    return high, x - high


def iota(shape, dim):
    return lax.broadcasted_iota(jnp.int32, shape, dim)


def cat(parts, axis):
    return parts[0] if len(parts) == 1 else jnp.concatenate(parts, axis=axis)


class Plan:
    def __init__(self, videos, rows, cols, frames, halves):
        self.videos, self.rows, self.cols = videos, rows, cols
        self.frames, self.halves = frames, halves
        self.chunks = frames // videos
        self.places = rows * cols // self.chunks
        self.qrows = max(1, self.places // cols)
        self.window = (self.qrows + 2 * REACH) * cols
        self.width = -(-(self.window + 3 * self.places) // LANES) * LANES
        self.tokens = frames * self.places
        self.low = LANES // frames
        self.stride = -(-(self.window + self.places) // LANES) * LANES
        self.marks = -(-(self.qrows + 2 * REACH) // 8) * 8
        self.qpad = -(-(HEAD_DIM + self.low) // 16) * 16
        whole = self.qrows * cols if self.places >= cols else cols
        assert frames % videos == 0 and (rows * cols) % self.chunks == 0
        assert self.places % cols == 0 or cols % self.places == 0
        assert rows >= REACH and rows % self.qrows == 0 and whole >= self.places
        for size in (cols, frames, self.places, self.low):
            assert size & (size - 1) == 0 and size > 0
        assert self.places % self.low == 0 and self.tokens % LANES == 0


def log_kept(step):
    counter = iota((8, LANES), 0) * LANES + iota((8, LANES), 1)
    beta = 0.0001 + (0.02 - 0.0001) * counter.astype(F32) / (STEPS - 1)
    used = (counter <= step) & (counter < STEPS)
    terms = jnp.where(used, jnp.log1p(-jnp.where(used, beta, 0.0)), 0.0)
    return jnp.sum(jnp.sum(terms, axis=0, keepdims=True), axis=1, keepdims=True)


def pack_kernel(plan, steps_ref, latents_ref, noise_ref, send_ref):
    half = lax.axis_index("row")
    channels = latents_ref.shape[2]
    videos = []
    for video in range(plan.videos):
        kept = jnp.exp(log_kept(steps_ref[video]))
        signal, spread = jnp.sqrt(kept), jnp.sqrt(1.0 - kept)
        noise = cat([noise_ref[video, row] for row in range(plan.rows)], 1)
        clean = cat([latents_ref[video, row] for row in range(plan.rows)], 1)
        videos.append((signal * clean + spread * noise, *split(noise)))

    def window(value, start, count):
        first, last = max(start, 0), min(start + count, plan.rows)
        if first >= last:
            return jnp.zeros((channels, count * plan.cols), F32)
        parts = []
        if first > start:
            parts.append(jnp.zeros((channels, (first - start) * plan.cols), F32))
        parts.append(value[:, first * plan.cols : last * plan.cols])
        if last < start + count:
            parts.append(jnp.zeros((channels, (start + count - last) * plan.cols), F32))
        return cat(parts, 1)

    unused = plan.width - plan.window - 3 * plan.places
    for target in range(plan.halves):
        for apart in range(1 - plan.halves, plan.halves):
            if not 0 <= target + apart < plan.halves:
                continue

            @pl.when(half == target + apart)
            def _():
                for peer in range(plan.frames):
                    values = videos[peer // plan.chunks]
                    place = (peer % plan.chunks) * plan.places
                    start = place // plan.cols - REACH - apart * plan.rows
                    parts = [window(values[0], start, plan.qrows + 2 * REACH)]
                    if apart == 0:
                        parts += [v[:, place : place + plan.places] for v in values]
                        if unused:
                            parts.append(jnp.zeros((channels, unused), F32))
                    else:
                        parts.append(jnp.zeros((channels, plan.width - plan.window), F32))
                    send_ref[peer * plan.halves + target] = cat(parts, 1).astype(BF16)


def fold_kernel(
    plan,
    steps_hbm,
    patch_hbm,
    time_hbm,
    sproject_hbm,
    soutput_hbm,
    tproject_hbm,
    toutput_hbm,
    gram_ref,
    score_ref,
    mixt_ref,
    query_ref,
    key_ref,
    value_ref,
    outt_ref,
    order_ref,
    rows_ref,
    steps_ref,
    patch_ref,
    time_ref,
    sproject_ref,
    soutput_ref,
    tproject_ref,
    toutput_ref,
    sems,
):
    model = patch_ref.shape[1]
    inner = soutput_ref.shape[0]
    halfway = time_ref.shape[0] // 2
    tokens, places, low = plan.tokens, plan.places, plan.low
    scale = math.log2(math.e) / math.sqrt(HEAD_DIM)
    parts = [slice(k * inner, (k + 1) * inner) for k in range(3)]
    pairs = [(time_hbm, time_ref), (patch_hbm, patch_ref)]
    pairs += [(sproject_hbm.at[cut], sproject_ref.at[cut]) for cut in parts]
    pairs += [(soutput_hbm, soutput_ref)]
    pairs += [(tproject_hbm.at[cut], tproject_ref.at[cut]) for cut in parts]
    pairs += [(toutput_hbm, toutput_ref), (steps_hbm, steps_ref)]
    copies = [
        pltpu.make_async_copy(source, target, sems.at[k])
        for k, (source, target) in enumerate(pairs)
    ]
    for copy in copies:
        copy.start()

    m = iota((tokens, tokens), 1)
    group, frame, place = m // LANES, (m & (LANES - 1)) // low, m & (low - 1)
    source = frame * places + group * low + place
    order_ref[...] = (iota((tokens, tokens), 0) == source).astype(BF16)

    half = lax.axis_index("row")
    chunk = lax.rem(lax.axis_index("frame"), plan.chunks)
    top = half * plan.rows + lax.div(chunk * places, plan.cols) - REACH
    key_row = iota((plan.marks, LANES), 0)
    query = iota((plan.marks, LANES), 1) & (places - 1)
    query_row = jnp.zeros((plan.marks, LANES), jnp.int32)
    for k in range(1, plan.qrows):
        query_row = query_row + (query >= k * plan.cols).astype(jnp.int32)
    seen = (key_row >= query_row) & (key_row <= query_row + 2 * REACH)
    seen = seen & (key_row + top >= 0) & (key_row + top < plan.halves * plan.rows)
    rows_ref[...] = jnp.where(seen, 0.0, -1e30)

    copies[10].wait()
    step = steps_ref[lax.axis_index("frame") // plan.chunks]
    freqs = jnp.exp(iota((8, halfway), 1).astype(F32) * (-math.log(10000.0) / halfway))
    angles = step.astype(F32) * freqs
    features = jnp.concatenate([jnp.cos(angles), jnp.sin(angles)], axis=1).astype(BF16)
    copies[0].wait()
    time_vector = dot(features, time_ref[...])
    time_rows = jnp.where(iota((8, model), 0) == 0, time_vector, 0.0)
    copies[1].wait()
    basis = jnp.concatenate([patch_ref[...].astype(F32), time_rows], axis=0)
    basis = basis - jnp.mean(basis, axis=1, keepdims=True)

    gram = dot(basis, basis, 1, 1, lax.Precision.HIGHEST) * (1.0 / model)
    high, rest = split(gram)
    middle, rest = split(rest)
    gram_ref[...] = jnp.concatenate([high, middle, rest], axis=0).astype(BF16)

    both = jnp.concatenate(split(basis), axis=0).astype(BF16)
    folded = []
    for k in range(3):
        copies[2 + k].wait()
        value = dot(both, sproject_ref[parts[k], :], 1, 1)
        folded.append(value[:BASIS] + value[BASIS:])
    queries, keys, values = folded
    lane = iota((BASIS, inner), 1)

    def by_head(value):
        return jnp.concatenate(
            [
                jnp.where((lane >= h * HEAD_DIM) & (lane < (h + 1) * HEAD_DIM), value, 0.0)
                for h in range(HEADS)
            ],
            axis=0,
        )

    score = dot(by_head(keys), queries * scale, 1, 1, lax.Precision.HIGHEST)
    high, rest = split(score)
    score_ref[...] = jnp.concatenate([high, high, rest], axis=1).astype(BF16)

    both = jnp.concatenate(split(by_head(values)), axis=0).astype(BF16)
    copies[5].wait()
    mixed = dot(both, soutput_ref[...])
    mixed = mixed[: HEADS * BASIS] + mixed[HEADS * BASIS :]
    mixed = mixed - jnp.mean(mixed, axis=1, keepdims=True)
    depth = mixt_ref.shape[1]
    used = (HEADS + 1) * BASIS
    whole = jnp.concatenate([basis, mixed, jnp.zeros((depth - used, model), F32)], axis=0)
    mixt_ref[...] = whole.T.astype(BF16)

    whole = whole.astype(BF16)
    folded = []
    for k in range(3):
        copies[6 + k].wait()
        folded.append(dot(tproject_ref[parts[k], :], whole, 1, 1))
    queries, keys, values = folded
    mark = iota((LANES - HEAD_DIM, depth), 1) - used
    row = iota((LANES - HEAD_DIM, depth), 0)
    placed = (mark >= 0) & (mark < low) & (row < low)
    key_mark = jnp.where(placed & (mark == row), 1.0, 0.0)
    query_mark = jnp.where(placed & (mark != row), -1e30, 0.0)[: plan.qpad - HEAD_DIM]
    blank = jnp.zeros((VPAD - HEAD_DIM, depth), F32)
    padded = []
    for h in range(HEADS):
        cut = slice(h * HEAD_DIM, (h + 1) * HEAD_DIM)
        padded += [keys[cut], key_mark]
        query_ref[pl.ds(h * plan.qpad, plan.qpad), :] = jnp.concatenate(
            [queries[cut] * scale, query_mark], axis=0
        ).astype(BF16)
        value_ref[pl.ds(h * VPAD, VPAD), :] = jnp.concatenate(
            [values[cut], blank], axis=0
        ).astype(BF16)
    key_ref[...] = jnp.concatenate(padded, axis=0).T.astype(BF16)

    copies[9].wait()
    output = toutput_ref[...].astype(F32)
    output = output - jnp.mean(output, axis=1, keepdims=True)
    outt_ref[...] = output.astype(BF16).T


def main_kernel(
    plan,
    recv_ref,
    gram_ref,
    score_ref,
    mixt_ref,
    query_ref,
    key_ref,
    value_ref,
    outt_ref,
    order_ref,
    rows_ref,
    finalt_ref,
    out_ref,
    mixed_ref,
    stream_ref,
):
    window, places, tokens = plan.window, plan.places, plan.tokens
    frames, stride = plan.frames, plan.stride
    channels = recv_ref.shape[1]
    depth = mixt_ref.shape[1]
    used = (HEADS + 1) * BASIS

    received = []
    for f in range(frames):
        value = recv_ref[f * plan.halves].astype(F32)
        for r in range(1, plan.halves):
            value = value + recv_ref[f * plan.halves + r].astype(F32)
        received.append(value)

    def query_lanes(values, k=0):
        return cat([v[:, window + k * places : window + (k + 1) * places] for v in values], 1)

    ones = (iota((BASIS - channels, frames * stride), 0) == 0).astype(F32)
    basis = jnp.concatenate([cat([v[:, :stride] for v in received], 1), ones], axis=0)
    image = dot(gram_ref[...], basis.astype(BF16))
    image = image[:BASIS] + image[BASIS : 2 * BASIS] + image[2 * BASIS :]
    variance = jnp.sum(basis * image, axis=0, keepdims=True)
    scaled = basis * lax.rsqrt(jnp.maximum(variance, 0.0) + EPS)
    high, rest = split(scaled)
    by_frame = [slice(f * stride, (f + 1) * stride) for f in range(frames)]
    qhigh, qrest = (query_lanes([v[:, cut] for cut in by_frame]) for v in (high, rest))
    turned = dot(score_ref[...], jnp.concatenate([qhigh, qrest, qhigh], axis=0).astype(BF16))
    qhigh, qrest = split(turned)

    packed = LANES // places
    starts = range(0, HEADS, packed)
    key_row = jnp.zeros((plan.marks, stride), jnp.int32)
    for k in range(1, window // plan.cols):
        key_row = key_row + (iota((plan.marks, stride), 1) >= k * plan.cols).astype(jnp.int32)
    marks = (iota((plan.marks, stride), 0) == key_row).astype(F32)
    count = (iota((8, window), 0) == 0).astype(F32)

    def gather(value, f, start):
        return cat(
            [
                value[h * BASIS : (h + 1) * BASIS, f * places : (f + 1) * places]
                for h in range(start, start + packed)
            ],
            1,
        )

    scores, lefts = [], []
    for f in range(frames):
        fhigh, frest = high[:, by_frame[f]], rest[:, by_frame[f]]
        left = jnp.concatenate([fhigh, fhigh, frest, marks], axis=0).T.astype(BF16)[:window]
        lefts.append(
            jnp.concatenate([fhigh[:, :window], frest[:, :window], count], axis=0).astype(BF16)
        )
        for start in starts:
            ahigh, arest = gather(qhigh, f, start), gather(qrest, f, start)
            right = jnp.concatenate([ahigh, arest, ahigh, rows_ref[...]], axis=0)
            scores.append(dot(left, right.astype(BF16)))
    weights = [
        jnp.exp2(score - jnp.max(score, axis=0, keepdims=True)).astype(BF16)
        for score in scores
    ]
    pieces = [[None] * frames for _ in range(HEADS)]
    for n, weight in enumerate(weights):
        f, start = n // len(starts), (n % len(starts)) * packed
        sums = dot(lefts[f], weight)
        mean = (sums[:BASIS] + sums[BASIS : 2 * BASIS]) / sums[2 * BASIS : 2 * BASIS + 1]
        for k in range(packed):
            pieces[start + k][f] = mean[:, k * places : (k + 1) * places]
    own = jnp.concatenate([query_lanes(received), ones[:, :tokens]], axis=0)
    combined = jnp.concatenate(
        [own]
        + [cat(piece, 1) for piece in pieces]
        + [jnp.zeros((depth - used, tokens), F32)]
        + [query_lanes(received, k) for k in (1, 2)],
        axis=0,
    ).astype(BF16)
    combined = dot(combined, order_ref[...])
    noise = combined[depth : depth + channels] + combined[depth + channels :]
    combined = combined[:depth]

    stream = dot(mixt_ref[...], combined.astype(BF16))
    stream_ref[...] = stream
    variance = jnp.mean(stream * stream, axis=0, keepdims=True)
    placed = (iota((depth - used, tokens), 1) & (plan.low - 1)) == iota((depth - used, tokens), 0)
    combined = jnp.concatenate(
        [combined[:used] * lax.rsqrt(variance + EPS), placed.astype(F32)], axis=0
    ).astype(BF16)
    keys = dot(combined, key_ref[...], 0, 0).astype(BF16)
    queries = dot(query_ref[...], combined).astype(BF16)
    units = [(slice(g, g + LANES), h) for g in range(0, tokens, LANES) for h in range(HEADS)]
    scores = [
        dot(
            keys[cut, h * LANES : h * LANES + plan.qpad],
            queries[h * plan.qpad : (h + 1) * plan.qpad, cut],
        )
        for cut, h in units
    ]
    values = dot(value_ref[...], combined).astype(BF16)
    weights, totals = [], []
    for score in scores:
        weight = jnp.exp2(score - jnp.max(score, axis=0, keepdims=True))
        totals.append(jnp.sum(weight, axis=0, keepdims=True))
        weights.append(weight.astype(BF16))
    for (cut, h), weight, total in zip(units, weights, totals):
        mean = dot(values[h * VPAD : (h + 1) * VPAD, cut], weight) / total
        mixed_ref[pl.ds(h * HEAD_DIM, HEAD_DIM), cut] = mean[:HEAD_DIM]

    stream = stream_ref[...] + dot(outt_ref[...], mixed_ref[...].astype(BF16))
    variance = jnp.mean(stream * stream, axis=0, keepdims=True)
    predicted = dot(finalt_ref[...], stream.astype(BF16)) * lax.rsqrt(variance + EPS)
    gap = predicted - noise
    errors = jnp.mean(gap * gap, axis=0, keepdims=True)
    high, rest = split(errors)
    middle, rest = split(rest)
    parts = jnp.concatenate([high, middle, rest] + [jnp.zeros_like(rest)] * 5, axis=0)
    errors = jnp.sum(dot(parts.astype(BF16), order_ref[...], 1, 1), axis=0, keepdims=True)
    lanes = out_ref.shape[1]
    for k in range(tokens // lanes):
        out_ref[pl.ds(k, 1), :] = errors[:, k * lanes : (k + 1) * lanes]


def grant(mib):
    return pltpu.CompilerParams(vmem_limit_bytes=mib << 20)


def near(value):
    return pltpu.with_memory_space_constraint(value, pltpu.VMEM)


def far(value):
    return pltpu.with_memory_space_constraint(value, pltpu.HBM)


def local(
    latents,
    target_noise,
    timesteps,
    patch_weight,
    time_weight,
    spatial_project,
    spatial_output,
    temporal_project,
    temporal_output,
    final_weight,
):
    videos, _, rows, cols, channels = latents.shape
    frames, halves = lax.axis_size("frame"), lax.axis_size("row")
    plan = Plan(videos, rows, cols, frames, halves)
    inner, model = spatial_output.shape
    depth = -(-(HEADS + 1) * BASIS // LANES) * LANES
    shape = jax.ShapeDtypeStruct

    def by_row(value):
        return value.reshape(videos, rows, cols, channels).transpose(0, 1, 3, 2)

    send = pl.pallas_call(
        functools.partial(pack_kernel, plan),
        out_shape=shape((frames * halves, channels, plan.width), BF16),
        in_specs=[SMEM, VMEM, VMEM],
        out_specs=VMEM,
    )(timesteps, by_row(latents), by_row(target_noise))
    received = lax.all_to_all(send, ("frame", "row"), 0, 0, tiled=True)

    weights = (
        patch_weight,
        time_weight,
        spatial_project.T,
        spatial_output,
        temporal_project.T,
        temporal_output,
    )
    tables = pl.pallas_call(
        functools.partial(fold_kernel, plan),
        out_shape=(
            pltpu.VMEM((3 * BASIS, BASIS), BF16),
            pltpu.VMEM((HEADS * BASIS, 3 * BASIS), BF16),
            pltpu.VMEM((model, depth), BF16),
            pltpu.VMEM((HEADS * plan.qpad, depth), BF16),
            pltpu.VMEM((depth, HEADS * LANES), BF16),
            pltpu.VMEM((HEADS * VPAD, depth), BF16),
            pltpu.VMEM((model, inner), BF16),
            pltpu.VMEM((plan.tokens, plan.tokens), BF16),
            pltpu.VMEM((plan.marks, LANES), F32),
        ),
        in_specs=[HBM] * (1 + len(weights)),
        out_specs=(VMEM,) * 9,
        scratch_shapes=[pltpu.SMEM(timesteps.shape, timesteps.dtype)]
        + [pltpu.VMEM(w.shape, w.dtype) for w in weights]
        + [pltpu.SemaphoreType.DMA((11,))],
        compiler_params=grant(26),
    )(*map(far, (timesteps, *weights)))

    lanes = min(plan.places, cols)
    errors = pl.pallas_call(
        functools.partial(main_kernel, plan),
        out_shape=shape((plan.tokens // lanes, lanes), F32),
        in_specs=[VMEM] * 11,
        out_specs=VMEM,
        compiler_params=grant(26),
        scratch_shapes=[
            pltpu.VMEM((inner, plan.tokens), F32),
            pltpu.VMEM((model, plan.tokens), F32),
        ],
    )(*map(near, (received, *tables)), final_weight.T)
    errors = lax.all_to_all(errors, "frame", 0, 0, tiled=True)
    return errors.reshape(videos, 1, rows, cols)


def solution(mesh):
    return jax.shard_map(
        local,
        mesh=mesh,
        in_specs=(
            P("grp", "frame", "row", None, None),
            P("grp", "frame", "row", None, None),
            P("grp"),
            P(),
            P(),
            P(),
            P(),
            P(),
            P(),
            P(),
        ),
        out_specs=P("grp", "frame", "row", None),
        check_vma=False,
    )
```

```python
import functools
import math

import jax
import jax.numpy as jnp
from jax import lax
from jax.experimental import pallas as pl
from jax.experimental.pallas import tpu as pltpu
from jax.sharding import PartitionSpec as P

HEAD_DIM = 72
HEADS = 8
STEPS = 1000
REACH = 2
EPS = 1e-06
LANES = 128
BASIS = 24
VPAD = 80
F32 = jnp.float32
BF16 = jnp.bfloat16
VMEM = pl.BlockSpec(memory_space=pltpu.VMEM)
SMEM = pl.BlockSpec(memory_space=pltpu.SMEM)
HBM = pl.BlockSpec(memory_space=pltpu.HBM)


def dot(a, b, ca=1, cb=0, precision=None):
    return lax.dot_general(
        a, b, (((ca,), (cb,)), ((), ())), preferred_element_type=F32, precision=precision
    )


def split(x):
    high = x.astype(BF16).astype(F32)
    return high, x - high


def iota(shape, dim):
    return lax.broadcasted_iota(jnp.int32, shape, dim)


def cat(parts, axis):
    return parts[0] if len(parts) == 1 else jnp.concatenate(parts, axis=axis)


class Plan:
    def __init__(self, videos, rows, cols, frames, halves):
        self.videos, self.rows, self.cols = videos, rows, cols
        self.frames, self.halves = frames, halves
        self.chunks = frames // videos
        self.places = rows * cols // self.chunks
        self.qrows = max(1, self.places // cols)
        self.window = (self.qrows + 2 * REACH) * cols
        self.width = -(-(self.window + 3 * self.places) // LANES) * LANES
        self.tokens = frames * self.places
        self.low = LANES // frames
        self.stride = -(-(self.window + self.places) // LANES) * LANES
        self.marks = -(-(self.qrows + 2 * REACH) // 8) * 8
        self.qpad = -(-(HEAD_DIM + self.low) // 16) * 16
        whole = self.qrows * cols if self.places >= cols else cols
        assert frames % videos == 0 and (rows * cols) % self.chunks == 0
        assert self.places % cols == 0 or cols % self.places == 0
        assert rows >= REACH and rows % self.qrows == 0 and whole >= self.places
        for size in (cols, frames, self.places, self.low):
            assert size & (size - 1) == 0 and size > 0
        assert self.places % self.low == 0 and self.tokens % LANES == 0


def log_kept(step):
    counter = iota((8, LANES), 0) * LANES + iota((8, LANES), 1)
    beta = 0.0001 + (0.02 - 0.0001) * counter.astype(F32) / (STEPS - 1)
    used = (counter <= step) & (counter < STEPS)
    terms = jnp.where(used, jnp.log1p(-jnp.where(used, beta, 0.0)), 0.0)
    return jnp.sum(jnp.sum(terms, axis=0, keepdims=True), axis=1, keepdims=True)


def pack_kernel(
    plan,
    steps_hbm,
    latents_hbm,
    noise_hbm,
    time_hbm,
    send_ref,
    time_ref,
    steps_ref,
    latents_ref,
    noise_ref,
    sems,
):
    pairs = [(steps_hbm, steps_ref), (latents_hbm, latents_ref), (noise_hbm, noise_ref)]
    pairs += [(time_hbm, time_ref)]
    copies = [
        pltpu.make_async_copy(source, target, sems.at[k])
        for k, (source, target) in enumerate(pairs)
    ]
    for copy in copies:
        copy.start()
    for copy in copies[:3]:
        copy.wait()
    half = lax.axis_index("row")
    channels = latents_ref.shape[2]
    videos = []
    for video in range(plan.videos):
        kept = jnp.exp(log_kept(steps_ref[video]))
        signal, spread = jnp.sqrt(kept), jnp.sqrt(1.0 - kept)
        noise = cat([noise_ref[video, row] for row in range(plan.rows)], 1)
        clean = cat([latents_ref[video, row] for row in range(plan.rows)], 1)
        videos.append((signal * clean + spread * noise, *split(noise)))

    def window(value, start, count):
        first, last = max(start, 0), min(start + count, plan.rows)
        if first >= last:
            return jnp.zeros((channels, count * plan.cols), F32)
        parts = []
        if first > start:
            parts.append(jnp.zeros((channels, (first - start) * plan.cols), F32))
        parts.append(value[:, first * plan.cols : last * plan.cols])
        if last < start + count:
            parts.append(jnp.zeros((channels, (start + count - last) * plan.cols), F32))
        return cat(parts, 1)

    unused = plan.width - plan.window - 3 * plan.places
    for target in range(plan.halves):
        for apart in range(1 - plan.halves, plan.halves):
            if not 0 <= target + apart < plan.halves:
                continue

            @pl.when(half == target + apart)
            def _():
                for peer in range(plan.frames):
                    values = videos[peer // plan.chunks]
                    place = (peer % plan.chunks) * plan.places
                    start = place // plan.cols - REACH - apart * plan.rows
                    parts = [window(values[0], start, plan.qrows + 2 * REACH)]
                    if apart == 0:
                        parts += [v[:, place : place + plan.places] for v in values]
                        if unused:
                            parts.append(jnp.zeros((channels, unused), F32))
                    else:
                        parts.append(jnp.zeros((channels, plan.width - plan.window), F32))
                    send_ref[peer * plan.halves + target] = cat(parts, 1).astype(BF16)
    copies[3].wait()


def fold_kernel(
    plan,
    time_ref,
    steps_hbm,
    patch_hbm,
    sproject_hbm,
    soutput_hbm,
    tproject_hbm,
    toutput_hbm,
    gram_ref,
    score_ref,
    mixt_ref,
    query_ref,
    key_ref,
    value_ref,
    outt_hbm,
    order_ref,
    rows_ref,
    steps_ref,
    patch_ref,
    sproject_ref,
    soutput_ref,
    tproject_ref,
    toutput_ref,
    outt_ref,
    sems,
):
    model = patch_ref.shape[1]
    inner = soutput_ref.shape[0]
    halfway = time_ref.shape[0] // 2
    tokens, places, low = plan.tokens, plan.places, plan.low
    scale = math.log2(math.e) / math.sqrt(HEAD_DIM)
    parts = [slice(k * inner, (k + 1) * inner) for k in range(3)]
    pairs = [(steps_hbm, steps_ref), (patch_hbm, patch_ref)]
    pairs += [(sproject_hbm.at[cut], sproject_ref.at[cut]) for cut in parts]
    pairs += [(soutput_hbm, soutput_ref), (toutput_hbm, toutput_ref)]
    pairs += [(tproject_hbm.at[cut], tproject_ref.at[cut]) for cut in parts]
    copies = [
        pltpu.make_async_copy(source, target, sems.at[k])
        for k, (source, target) in enumerate(pairs)
    ]
    for copy in copies:
        copy.start()

    lane = iota(order_ref.shape, 1)
    row = iota(order_ref.shape, 0) - (places // low - 1) * low
    order_ref[...] = (row == (lane // low) * places + (lane & (low - 1))).astype(BF16)

    half = lax.axis_index("row")
    chunk = lax.rem(lax.axis_index("frame"), plan.chunks)
    top = half * plan.rows + lax.div(chunk * places, plan.cols) - REACH
    key_row = iota((plan.marks, LANES), 0)
    query = iota((plan.marks, LANES), 1) & (places - 1)
    query_row = jnp.zeros((plan.marks, LANES), jnp.int32)
    for k in range(1, plan.qrows):
        query_row = query_row + (query >= k * plan.cols).astype(jnp.int32)
    seen = (key_row >= query_row) & (key_row <= query_row + 2 * REACH)
    seen = seen & (key_row + top >= 0) & (key_row + top < plan.halves * plan.rows)
    rows_ref[...] = jnp.where(seen, 0.0, -1e30)

    copies[0].wait()
    step = steps_ref[lax.axis_index("frame") // plan.chunks]
    freqs = jnp.exp(iota((8, halfway), 1).astype(F32) * (-math.log(10000.0) / halfway))
    angles = step.astype(F32) * freqs
    features = jnp.concatenate([jnp.cos(angles), jnp.sin(angles)], axis=1).astype(BF16)
    time_vector = dot(features, time_ref[...])
    time_rows = jnp.where(iota((8, model), 0) == 0, time_vector, 0.0)
    copies[1].wait()
    basis = jnp.concatenate([patch_ref[...].astype(F32), time_rows], axis=0)
    basis = basis - jnp.mean(basis, axis=1, keepdims=True)

    gram = dot(basis, basis, 1, 1, lax.Precision.HIGHEST) * (1.0 / model)
    high, rest = split(gram)
    middle, rest = split(rest)
    gram_ref[...] = jnp.concatenate([high, middle, rest], axis=0).astype(BF16)

    both = jnp.concatenate(split(basis), axis=0).astype(BF16)
    folded = []
    for k in range(3):
        copies[2 + k].wait()
        value = dot(both, sproject_ref[parts[k], :], 1, 1)
        folded.append(value[:BASIS] + value[BASIS:])
    queries, keys, values = folded
    lane = iota((BASIS, inner), 1)

    def by_head(value):
        return jnp.concatenate(
            [
                jnp.where((lane >= h * HEAD_DIM) & (lane < (h + 1) * HEAD_DIM), value, 0.0)
                for h in range(HEADS)
            ],
            axis=0,
        )

    score = dot(by_head(keys), queries * scale, 1, 1, lax.Precision.HIGHEST)
    high, rest = split(score)
    score_ref[...] = jnp.concatenate([high, high, rest], axis=1).astype(BF16)

    both = jnp.concatenate(split(by_head(values)), axis=0).astype(BF16)
    copies[5].wait()
    mixed = dot(both, soutput_ref[...])
    mixed = mixed[: HEADS * BASIS] + mixed[HEADS * BASIS :]
    mixed = mixed - jnp.mean(mixed, axis=1, keepdims=True)
    copies[6].wait()
    average = dot(jnp.ones((8, model), BF16), toutput_ref[...], 1, 1)[:1] * (1.0 / model)
    high, rest = split(average)
    outt_ref[pl.ds(16, model), :] = toutput_ref[...].T
    outt_ref[pl.ds(0, 16), :] = jnp.concatenate(
        [high, rest, jnp.zeros((14, inner), F32)], axis=0
    ).astype(BF16)
    outt_copy = pltpu.make_async_copy(outt_ref, outt_hbm, sems.at[10])
    outt_copy.start()

    depth = mixt_ref.shape[1]
    used = (HEADS + 1) * BASIS
    whole = jnp.concatenate([basis, mixed, jnp.zeros((depth - used, model), F32)], axis=0)
    whole = whole.astype(BF16)
    mixt_ref[...] = whole.T

    folded = []
    for k in range(3):
        copies[7 + k].wait()
        folded.append(dot(tproject_ref[parts[k], :], whole, 1, 1))
    queries, keys, values = folded
    mark = iota((LANES - HEAD_DIM, depth), 1) - used
    row = iota((LANES - HEAD_DIM, depth), 0)
    placed = (mark >= 0) & (mark < low) & (row < low)
    key_mark = jnp.where(placed & (mark == row), 1.0, 0.0)
    query_mark = jnp.where(placed & (mark != row), -1e30, 0.0)[: plan.qpad - HEAD_DIM]
    blank = jnp.zeros((VPAD - HEAD_DIM, depth), F32)
    padded = []
    for h in range(HEADS):
        cut = slice(h * HEAD_DIM, (h + 1) * HEAD_DIM)
        padded += [keys[cut], key_mark]
        query_ref[pl.ds(h * plan.qpad, plan.qpad), :] = jnp.concatenate(
            [queries[cut] * scale, query_mark], axis=0
        ).astype(BF16)
        value_ref[pl.ds(h * VPAD, VPAD), :] = jnp.concatenate(
            [values[cut], blank], axis=0
        ).astype(BF16)
    key_ref[...] = jnp.concatenate(padded, axis=0).astype(BF16).T
    outt_copy.wait()


def main_kernel(
    plan,
    recv_ref,
    gram_ref,
    score_ref,
    mixt_ref,
    query_ref,
    key_ref,
    value_ref,
    outt_hbm,
    order_ref,
    rows_ref,
    finalt_ref,
    out_ref,
    mixed_ref,
    stream_ref,
    outt_ref,
    total_ref,
    sem,
):
    window, places, tokens = plan.window, plan.places, plan.tokens
    frames, stride = plan.frames, plan.stride
    channels = recv_ref.shape[1]
    depth = mixt_ref.shape[1]
    used = (HEADS + 1) * BASIS

    outt_copy = pltpu.make_async_copy(outt_hbm, outt_ref, sem)
    outt_copy.start()
    groups = range(places // plan.low)
    order = cat(
        [order_ref[pl.ds((len(groups) - 1 - k) * plan.low, tokens), :] for k in groups], 1
    )

    def add(f, carry):
        value = recv_ref[f * plan.halves].astype(F32)
        for r in range(1, plan.halves):
            value = value + recv_ref[f * plan.halves + r].astype(F32)
        total_ref[f] = value
        return carry

    lax.fori_loop(0, frames, add, 0)
    received = [total_ref[f] for f in range(frames)]

    def query_lanes(values, k=0):
        return cat([v[:, window + k * places : window + (k + 1) * places] for v in values], 1)

    ones = (iota((BASIS - channels, frames * stride), 0) == 0).astype(F32)
    basis = jnp.concatenate([cat([v[:, :stride] for v in received], 1), ones], axis=0)
    image = dot(gram_ref[...], basis.astype(BF16))
    image = image[:BASIS] + image[BASIS : 2 * BASIS] + image[2 * BASIS :]
    variance = jnp.sum(basis * image, axis=0, keepdims=True)
    scaled = basis * lax.rsqrt(jnp.maximum(variance, 0.0) + EPS)
    high, rest = split(scaled)
    by_frame = [slice(f * stride, (f + 1) * stride) for f in range(frames)]
    qhigh, qrest = (query_lanes([v[:, cut] for cut in by_frame]) for v in (high, rest))
    turned = dot(score_ref[...], jnp.concatenate([qhigh, qrest, qhigh], axis=0).astype(BF16))
    qhigh, qrest = split(turned)

    packed = LANES // places
    starts = range(0, HEADS, packed)
    key_row = jnp.zeros((plan.marks, stride), jnp.int32)
    for k in range(1, window // plan.cols):
        key_row = key_row + (iota((plan.marks, stride), 1) >= k * plan.cols).astype(jnp.int32)
    marks = (iota((plan.marks, stride), 0) == key_row).astype(F32)
    count = (iota((8, window), 0) == 0).astype(F32)

    def gather(value, f, start):
        return cat(
            [
                value[h * BASIS : (h + 1) * BASIS, f * places : (f + 1) * places]
                for h in range(start, start + packed)
            ],
            1,
        )

    scores, lefts = [], []
    for f in range(frames):
        fhigh, frest = high[:, by_frame[f]], rest[:, by_frame[f]]
        left = jnp.concatenate([fhigh, fhigh, frest, marks], axis=0).T.astype(BF16)[:window]
        lefts.append(
            jnp.concatenate([fhigh[:, :window], frest[:, :window], count], axis=0).astype(BF16)
        )
        for start in starts:
            ahigh, arest = gather(qhigh, f, start), gather(qrest, f, start)
            right = jnp.concatenate([ahigh, arest, ahigh, rows_ref[...]], axis=0)
            scores.append(dot(left, right.astype(BF16)))
    weights = [
        jnp.exp2(score - jnp.max(score, axis=0, keepdims=True)).astype(BF16)
        for score in scores
    ]
    pieces = [[None] * frames for _ in range(HEADS)]
    for n, weight in enumerate(weights):
        f, start = n // len(starts), (n % len(starts)) * packed
        sums = dot(lefts[f], weight)
        mean = (sums[:BASIS] + sums[BASIS : 2 * BASIS]) / sums[2 * BASIS : 2 * BASIS + 1]
        for k in range(packed):
            pieces[start + k][f] = mean[:, k * places : (k + 1) * places]
    own = jnp.concatenate([query_lanes(received), ones[:, :tokens]], axis=0)
    combined = jnp.concatenate(
        [own]
        + [cat(piece, 1) for piece in pieces]
        + [jnp.zeros((depth - used, tokens), F32)]
        + [query_lanes(received, k) for k in (1, 2)],
        axis=0,
    ).astype(BF16)
    combined = dot(combined, order)
    noise = combined[depth : depth + channels] + combined[depth + channels :]
    combined = combined[:depth]

    stream = dot(mixt_ref[...], combined.astype(BF16))
    stream_ref[...] = stream
    variance = jnp.mean(stream * stream, axis=0, keepdims=True)
    placed = (iota((depth - used, tokens), 1) & (plan.low - 1)) == iota((depth - used, tokens), 0)
    combined = jnp.concatenate(
        [combined[:used] * lax.rsqrt(variance + EPS), placed.astype(F32)], axis=0
    ).astype(BF16)
    keys = dot(combined, key_ref[...], 0, 0).astype(BF16)
    queries = dot(query_ref[...], combined).astype(BF16)
    units = [(slice(g, g + LANES), h) for g in range(0, tokens, LANES) for h in range(HEADS)]
    scores = [
        dot(
            keys[cut, h * LANES : h * LANES + plan.qpad],
            queries[h * plan.qpad : (h + 1) * plan.qpad, cut],
        )
        for cut, h in units
    ]
    values = dot(value_ref[...], combined).astype(BF16)
    weights, totals = [], []
    for score in scores:
        weight = jnp.exp2(score - jnp.max(score, axis=0, keepdims=True))
        totals.append(jnp.sum(weight, axis=0, keepdims=True))
        weights.append(weight.astype(BF16))
    for (cut, h), weight, total in zip(units, weights, totals):
        mean = dot(values[h * VPAD : (h + 1) * VPAD, cut], weight) / total
        mixed_ref[pl.ds(h * HEAD_DIM, HEAD_DIM), cut] = mean[:HEAD_DIM]

    outt_copy.wait()
    delta = dot(outt_ref[...], mixed_ref[...].astype(BF16))
    average = delta[:1] + delta[1:2]
    stream = (stream_ref[...] - average) + delta[16:]
    variance = jnp.mean(stream * stream, axis=0, keepdims=True)
    predicted = dot(finalt_ref[...], stream.astype(BF16)) * lax.rsqrt(variance + EPS)
    gap = predicted - noise
    errors = jnp.mean(gap * gap, axis=0, keepdims=True)
    high, rest = split(errors)
    middle, rest = split(rest)
    parts = jnp.concatenate([high, middle, rest] + [jnp.zeros_like(rest)] * 5, axis=0)
    errors = jnp.sum(dot(parts.astype(BF16), order, 1, 1), axis=0, keepdims=True)
    lanes = out_ref.shape[1]
    for k in range(tokens // lanes):
        out_ref[pl.ds(k, 1), :] = errors[:, k * lanes : (k + 1) * lanes]


def grant(mib):
    return pltpu.CompilerParams(vmem_limit_bytes=mib << 20)


def near(value):
    return pltpu.with_memory_space_constraint(value, pltpu.VMEM)


def far(value):
    return pltpu.with_memory_space_constraint(value, pltpu.HBM)


def local(
    latents,
    target_noise,
    timesteps,
    patch_weight,
    time_weight,
    spatial_project,
    spatial_output,
    temporal_project,
    temporal_output,
    final_weight,
):
    videos, _, rows, cols, channels = latents.shape
    frames, halves = lax.axis_size("frame"), lax.axis_size("row")
    plan = Plan(videos, rows, cols, frames, halves)
    inner, model = spatial_output.shape
    depth = -(-(HEADS + 1) * BASIS // LANES) * LANES
    shape = jax.ShapeDtypeStruct

    def by_row(value):
        return value.reshape(videos, rows, cols, channels).transpose(0, 1, 3, 2)

    send, time_near = pl.pallas_call(
        functools.partial(pack_kernel, plan),
        out_shape=(
            pltpu.VMEM((frames * halves, channels, plan.width), BF16),
            pltpu.VMEM(time_weight.shape, time_weight.dtype),
        ),
        in_specs=[HBM] * 4,
        out_specs=(VMEM,) * 2,
        compiler_params=grant(26),
        scratch_shapes=[
            pltpu.SMEM(timesteps.shape, timesteps.dtype),
            pltpu.VMEM((videos, rows, channels, cols), F32),
            pltpu.VMEM((videos, rows, channels, cols), F32),
            pltpu.SemaphoreType.DMA((4,)),
        ],
    )(*map(far, (timesteps, by_row(latents), by_row(target_noise), time_weight)))
    received = lax.all_to_all(send, ("frame", "row"), 0, 0, tiled=True)

    weights = (
        patch_weight,
        spatial_project.T,
        spatial_output,
        temporal_project.T,
        temporal_output,
    )
    tables = pl.pallas_call(
        functools.partial(fold_kernel, plan),
        out_shape=(
            pltpu.VMEM((3 * BASIS, BASIS), BF16),
            pltpu.VMEM((HEADS * BASIS, 3 * BASIS), BF16),
            pltpu.VMEM((model, depth), BF16),
            pltpu.VMEM((HEADS * plan.qpad, depth), BF16),
            pltpu.VMEM((depth, HEADS * LANES), BF16),
            pltpu.VMEM((HEADS * VPAD, depth), BF16),
            pltpu.HBM((model + 16, inner), BF16),
            pltpu.VMEM((plan.tokens + plan.places - plan.low, LANES), BF16),
            pltpu.VMEM((plan.marks, LANES), F32),
        ),
        in_specs=[VMEM] + [HBM] * (1 + len(weights)),
        out_specs=(VMEM,) * 6 + (HBM,) + (VMEM,) * 2,
        scratch_shapes=[pltpu.SMEM(timesteps.shape, timesteps.dtype)]
        + [pltpu.VMEM(w.shape, w.dtype) for w in weights]
        + [pltpu.VMEM((model + 16, inner), BF16), pltpu.SemaphoreType.DMA((11,))],
        compiler_params=grant(26),
    )(near(time_near), *map(far, (timesteps, *weights)))

    outt = tables[6]
    lanes = min(plan.places, cols)
    errors = pl.pallas_call(
        functools.partial(main_kernel, plan),
        out_shape=shape((plan.tokens // lanes, lanes), F32),
        in_specs=[VMEM] * 7 + [HBM] + [VMEM] * 3,
        out_specs=VMEM,
        compiler_params=grant(26),
        scratch_shapes=[
            pltpu.VMEM((inner, plan.tokens), F32),
            pltpu.VMEM((model, plan.tokens), F32),
            pltpu.VMEM(outt.shape, outt.dtype),
            pltpu.VMEM((frames, channels, plan.width), F32),
            pltpu.SemaphoreType.DMA,
        ],
    )(
        *map(near, (received, *tables[:6])),
        far(outt),
        *map(near, (*tables[7:], final_weight.T)),
    )
    errors = lax.all_to_all(errors, "frame", 0, 0, tiled=True)
    return errors.reshape(videos, 1, rows, cols)


def solution(mesh):
    return jax.shard_map(
        local,
        mesh=mesh,
        in_specs=(
            P("grp", "frame", "row", None, None),
            P("grp", "frame", "row", None, None),
            P("grp"),
            P(),
            P(),
            P(),
            P(),
            P(),
            P(),
            P(),
        ),
        out_specs=P("grp", "frame", "row", None),
        check_vma=False,
    )
```

```python
import functools
import math

import jax
import jax.numpy as jnp
from jax import lax
from jax.experimental import pallas as pl
from jax.experimental.pallas import tpu as pltpu
from jax.sharding import PartitionSpec as P

HEAD_DIM = 72
HEADS = 8
STEPS = 1000
REACH = 2
EPS = 1e-06
LANES = 128
BASIS = 24
VPAD = 80
F32 = jnp.float32
BF16 = jnp.bfloat16
VMEM = pl.BlockSpec(memory_space=pltpu.VMEM)
SMEM = pl.BlockSpec(memory_space=pltpu.SMEM)
HBM = pl.BlockSpec(memory_space=pltpu.HBM)


def dot(a, b, ca=1, cb=0, precision=None):
    return lax.dot_general(
        a, b, (((ca,), (cb,)), ((), ())), preferred_element_type=F32, precision=precision
    )


def split(x):
    high = x.astype(BF16).astype(F32)
    return high, x - high


def iota(shape, dim):
    return lax.broadcasted_iota(jnp.int32, shape, dim)


def cat(parts, axis):
    return parts[0] if len(parts) == 1 else jnp.concatenate(parts, axis=axis)


class Plan:
    def __init__(self, videos, rows, cols, frames, halves):
        self.videos, self.rows, self.cols = videos, rows, cols
        self.frames, self.halves = frames, halves
        self.chunks = frames // videos
        self.places = rows * cols // self.chunks
        self.qrows = max(1, self.places // cols)
        self.window = (self.qrows + 2 * REACH) * cols
        self.width = -(-(self.window + 3 * self.places) // LANES) * LANES
        self.tokens = frames * self.places
        self.low = LANES // frames
        self.stride = -(-(self.window + self.places) // LANES) * LANES
        self.marks = -(-(self.qrows + 2 * REACH) // 8) * 8
        self.qpad = -(-(HEAD_DIM + self.low) // 16) * 16
        whole = self.qrows * cols if self.places >= cols else cols
        assert frames % videos == 0 and (rows * cols) % self.chunks == 0
        assert self.places % cols == 0 or cols % self.places == 0
        assert rows >= REACH and rows % self.qrows == 0 and whole >= self.places
        for size in (cols, frames, self.places, self.low):
            assert size & (size - 1) == 0 and size > 0
        assert self.places % self.low == 0 and self.tokens % LANES == 0


def log_kept(step):
    counter = iota((8, LANES), 0) * LANES + iota((8, LANES), 1)
    beta = 0.0001 + (0.02 - 0.0001) * counter.astype(F32) / (STEPS - 1)
    used = (counter <= step) & (counter < STEPS)
    terms = jnp.where(used, jnp.log1p(-jnp.where(used, beta, 0.0)), 0.0)
    return jnp.sum(jnp.sum(terms, axis=0, keepdims=True), axis=1, keepdims=True)


def pack_kernel(
    plan,
    steps_hbm,
    latents_hbm,
    noise_hbm,
    time_hbm,
    send_ref,
    time_ref,
    steps_ref,
    latents_ref,
    noise_ref,
    sems,
):
    pairs = [(steps_hbm, steps_ref), (latents_hbm, latents_ref), (noise_hbm, noise_ref)]
    pairs += [(time_hbm, time_ref)]
    copies = [
        pltpu.make_async_copy(source, target, sems.at[k])
        for k, (source, target) in enumerate(pairs)
    ]
    for copy in copies:
        copy.start()
    for copy in copies[:3]:
        copy.wait()
    half = lax.axis_index("row")
    channels = latents_ref.shape[2]
    videos = []
    for video in range(plan.videos):
        kept = jnp.exp(log_kept(steps_ref[video]))
        signal, spread = jnp.sqrt(kept), jnp.sqrt(1.0 - kept)
        noise = cat([noise_ref[video, row] for row in range(plan.rows)], 1)
        clean = cat([latents_ref[video, row] for row in range(plan.rows)], 1)
        videos.append((signal * clean + spread * noise, *split(noise)))

    def window(value, start, count):
        first, last = max(start, 0), min(start + count, plan.rows)
        if first >= last:
            return jnp.zeros((channels, count * plan.cols), F32)
        parts = []
        if first > start:
            parts.append(jnp.zeros((channels, (first - start) * plan.cols), F32))
        parts.append(value[:, first * plan.cols : last * plan.cols])
        if last < start + count:
            parts.append(jnp.zeros((channels, (start + count - last) * plan.cols), F32))
        return cat(parts, 1)

    unused = plan.width - plan.window - 3 * plan.places
    for target in range(plan.halves):
        for apart in range(1 - plan.halves, plan.halves):
            if not 0 <= target + apart < plan.halves:
                continue

            @pl.when(half == target + apart)
            def _():
                for peer in range(plan.frames):
                    values = videos[peer // plan.chunks]
                    place = (peer % plan.chunks) * plan.places
                    start = place // plan.cols - REACH - apart * plan.rows
                    parts = [window(values[0], start, plan.qrows + 2 * REACH)]
                    if apart == 0:
                        parts += [v[:, place : place + plan.places] for v in values]
                        if unused:
                            parts.append(jnp.zeros((channels, unused), F32))
                    else:
                        parts.append(jnp.zeros((channels, plan.width - plan.window), F32))
                    send_ref[peer * plan.halves + target] = cat(parts, 1).astype(BF16)
    copies[3].wait()


def fold_kernel(
    plan,
    time_ref,
    steps_hbm,
    patch_hbm,
    sproject_hbm,
    soutput_hbm,
    tproject_hbm,
    toutput_hbm,
    gram_ref,
    score_ref,
    mixt_ref,
    query_ref,
    key_ref,
    value_ref,
    outt_hbm,
    order_ref,
    rows_ref,
    steps_ref,
    patch_ref,
    sproject_ref,
    soutput_ref,
    tproject_ref,
    toutput_ref,
    outt_ref,
    sems,
):
    model = patch_ref.shape[1]
    inner = soutput_ref.shape[0]
    halfway = time_ref.shape[0] // 2
    tokens, places, low = plan.tokens, plan.places, plan.low
    scale = math.log2(math.e) / math.sqrt(HEAD_DIM)
    parts = [slice(k * inner, (k + 1) * inner) for k in range(3)]
    pairs = [(steps_hbm, steps_ref), (patch_hbm, patch_ref), (toutput_hbm, toutput_ref)]
    pairs += [(sproject_hbm.at[cut], sproject_ref.at[cut]) for cut in parts]
    pairs += [(soutput_hbm, soutput_ref)]
    pairs += [(tproject_hbm.at[cut], tproject_ref.at[cut]) for cut in parts]
    copies = [
        pltpu.make_async_copy(source, target, sems.at[k])
        for k, (source, target) in enumerate(pairs)
    ]
    for copy in copies:
        copy.start()

    lane = iota(order_ref.shape, 1)
    row = iota(order_ref.shape, 0) - (places // low - 1) * low
    order_ref[...] = (row == (lane // low) * places + (lane & (low - 1))).astype(BF16)

    half = lax.axis_index("row")
    chunk = lax.rem(lax.axis_index("frame"), plan.chunks)
    top = half * plan.rows + lax.div(chunk * places, plan.cols) - REACH
    key_row = iota((plan.marks, LANES), 0)
    query = iota((plan.marks, LANES), 1) & (places - 1)
    query_row = jnp.zeros((plan.marks, LANES), jnp.int32)
    for k in range(1, plan.qrows):
        query_row = query_row + (query >= k * plan.cols).astype(jnp.int32)
    seen = (key_row >= query_row) & (key_row <= query_row + 2 * REACH)
    seen = seen & (key_row + top >= 0) & (key_row + top < plan.halves * plan.rows)
    rows_ref[...] = jnp.where(seen, 0.0, -1e30)

    copies[0].wait()
    step = steps_ref[lax.axis_index("frame") // plan.chunks]
    freqs = jnp.exp(iota((8, halfway), 1).astype(F32) * (-math.log(10000.0) / halfway))
    angles = step.astype(F32) * freqs
    features = jnp.concatenate([jnp.cos(angles), jnp.sin(angles)], axis=1).astype(BF16)
    time_vector = dot(features, time_ref[...])
    time_rows = jnp.where(iota((8, model), 0) == 0, time_vector, 0.0)
    copies[1].wait()
    basis = jnp.concatenate([patch_ref[...].astype(F32), time_rows], axis=0)
    basis = basis - jnp.mean(basis, axis=1, keepdims=True)

    gram = dot(basis, basis, 1, 1, lax.Precision.HIGHEST) * (1.0 / model)
    high, rest = split(gram)
    middle, rest = split(rest)
    gram_ref[...] = jnp.concatenate([high, middle, rest], axis=0).astype(BF16)

    copies[2].wait()
    average = dot(jnp.ones((8, model), BF16), toutput_ref[...], 1, 1)[:1] * (1.0 / model)
    high, rest = split(average)
    outt_ref[pl.ds(16, model), :] = toutput_ref[...].T
    outt_ref[pl.ds(0, 16), :] = jnp.concatenate(
        [high, rest, jnp.zeros((14, inner), F32)], axis=0
    ).astype(BF16)
    outt_copy = pltpu.make_async_copy(outt_ref, outt_hbm, sems.at[10])
    outt_copy.start()

    both = jnp.concatenate(split(basis), axis=0).astype(BF16)
    folded = []
    for k in range(3):
        copies[3 + k].wait()
        value = dot(both, sproject_ref[parts[k], :], 1, 1)
        folded.append(value[:BASIS] + value[BASIS:])
    queries, keys, values = folded
    def by_head(value, first, count):
        lane = iota(value.shape, 1)
        return [
            jnp.where((lane >= h * HEAD_DIM) & (lane < (h + 1) * HEAD_DIM), value, 0.0)
            for h in range(first, first + count)
        ]

    khigh, krest = (
        jnp.concatenate(by_head(v, 0, HEADS), axis=0).astype(BF16) for v in split(keys)
    )
    qhigh, qrest = split(queries * scale)
    both = dot(jnp.concatenate([qhigh, qrest], axis=0).astype(BF16), khigh, 1, 1)
    score = both[:BASIS] + both[BASIS:] + dot(qhigh.astype(BF16), krest, 1, 1)
    unused = jnp.zeros((LANES - BASIS, HEADS * BASIS), F32)
    high, rest = split(jnp.concatenate([score, unused], axis=0).T[:, :BASIS])
    score_ref[...] = jnp.concatenate([high, high, rest], axis=1).astype(BF16)

    copies[6].wait()
    group = 2 if (2 * HEAD_DIM) % 16 == 0 else HEADS
    mixed = []
    for first in range(0, HEADS, group):
        cut = slice(first * HEAD_DIM, (first + group) * HEAD_DIM)
        both = jnp.concatenate(
            [part for v in split(values[:, cut]) for part in by_head(v, 0, group)], axis=0
        )
        both = dot(both.astype(BF16), soutput_ref[cut, :])
        mixed.append(both[: group * BASIS] + both[group * BASIS :])
    mixed = jnp.concatenate(mixed, axis=0)
    mixed = mixed - jnp.mean(mixed, axis=1, keepdims=True)
    depth = mixt_ref.shape[1]
    used = (HEADS + 1) * BASIS
    whole = jnp.concatenate([basis, mixed, jnp.zeros((depth - used, model), F32)], axis=0)
    whole = whole.astype(BF16)
    mixt_ref[...] = whole.T

    folded = []
    for k in range(3):
        copies[7 + k].wait()
        folded.append(dot(tproject_ref[parts[k], :], whole, 1, 1))
    queries, keys, values = folded
    mark = iota((LANES - HEAD_DIM, depth), 1) - used
    row = iota((LANES - HEAD_DIM, depth), 0)
    placed = (mark >= 0) & (mark < low) & (row < low)
    key_mark = jnp.where(placed & (mark == row), 1.0, 0.0)
    query_mark = jnp.where(placed & (mark != row), -1e30, 0.0)[: plan.qpad - HEAD_DIM]
    blank = jnp.zeros((VPAD - HEAD_DIM, depth), F32)
    padded = []
    for h in range(HEADS):
        cut = slice(h * HEAD_DIM, (h + 1) * HEAD_DIM)
        padded += [keys[cut], key_mark]
        query_ref[pl.ds(h * plan.qpad, plan.qpad), :] = jnp.concatenate(
            [queries[cut] * scale, query_mark], axis=0
        ).astype(BF16)
        value_ref[pl.ds(h * VPAD, VPAD), :] = jnp.concatenate(
            [values[cut], blank], axis=0
        ).astype(BF16)
    key_ref[...] = jnp.concatenate(padded, axis=0).astype(BF16).T
    outt_copy.wait()


def main_kernel(
    plan,
    recv_ref,
    gram_ref,
    score_ref,
    mixt_ref,
    query_ref,
    key_ref,
    value_ref,
    outt_hbm,
    order_ref,
    rows_ref,
    finalt_ref,
    out_ref,
    mixed_ref,
    stream_ref,
    outt_ref,
    total_ref,
    sem,
):
    window, places, tokens = plan.window, plan.places, plan.tokens
    frames, stride = plan.frames, plan.stride
    channels = recv_ref.shape[1]
    depth = mixt_ref.shape[1]
    used = (HEADS + 1) * BASIS

    outt_copy = pltpu.make_async_copy(outt_hbm, outt_ref, sem)
    outt_copy.start()
    groups = range(places // plan.low)
    order = cat(
        [order_ref[pl.ds((len(groups) - 1 - k) * plan.low, tokens), :] for k in groups], 1
    )

    def add(f, carry):
        value = recv_ref[f * plan.halves].astype(F32)
        for r in range(1, plan.halves):
            value = value + recv_ref[f * plan.halves + r].astype(F32)
        total_ref[f] = value
        return carry

    lax.fori_loop(0, frames, add, 0)
    received = [total_ref[f] for f in range(frames)]

    def query_lanes(values, k=0):
        return cat([v[:, window + k * places : window + (k + 1) * places] for v in values], 1)

    ones = (iota((BASIS - channels, frames * stride), 0) == 0).astype(F32)
    basis = jnp.concatenate([cat([v[:, :stride] for v in received], 1), ones], axis=0)
    image = dot(gram_ref[...], basis.astype(BF16))
    image = image[:BASIS] + image[BASIS : 2 * BASIS] + image[2 * BASIS :]
    variance = jnp.sum(basis * image, axis=0, keepdims=True)
    scaled = basis * lax.rsqrt(jnp.maximum(variance, 0.0) + EPS)
    high, rest = split(scaled)
    by_frame = [slice(f * stride, (f + 1) * stride) for f in range(frames)]
    qhigh, qrest = (query_lanes([v[:, cut] for cut in by_frame]) for v in (high, rest))
    turned = dot(score_ref[...], jnp.concatenate([qhigh, qrest, qhigh], axis=0).astype(BF16))
    qhigh, qrest = split(turned)

    packed = min(HEADS, 2 * LANES // places)
    sides = cat([rows_ref[...]] * (packed * places // LANES), 1)
    starts = range(0, HEADS, packed)
    key_row = jnp.zeros((plan.marks, stride), jnp.int32)
    for k in range(1, window // plan.cols):
        key_row = key_row + (iota((plan.marks, stride), 1) >= k * plan.cols).astype(jnp.int32)
    marks = (iota((plan.marks, stride), 0) == key_row).astype(F32)
    count = (iota((8, window), 0) == 0).astype(F32)

    def gather(value, f, start):
        return cat(
            [
                value[h * BASIS : (h + 1) * BASIS, f * places : (f + 1) * places]
                for h in range(start, start + packed)
            ],
            1,
        )

    scores, lefts = [], []
    for f in range(frames):
        fhigh, frest = high[:, by_frame[f]], rest[:, by_frame[f]]
        left = jnp.concatenate([fhigh, fhigh, frest, marks], axis=0).T.astype(BF16)[:window]
        lefts.append(
            jnp.concatenate([fhigh[:, :window], frest[:, :window], count], axis=0).astype(BF16)
        )
        for start in starts:
            ahigh, arest = gather(qhigh, f, start), gather(qrest, f, start)
            right = jnp.concatenate([ahigh, arest, ahigh, sides], axis=0)
            scores.append(dot(left, right.astype(BF16)))
    weights = [
        jnp.exp2(score - jnp.max(score, axis=0, keepdims=True)).astype(BF16)
        for score in scores
    ]
    pieces = [[None] * frames for _ in range(HEADS)]
    for n, weight in enumerate(weights):
        f, start = n // len(starts), (n % len(starts)) * packed
        sums = dot(lefts[f], weight)
        mean = (sums[:BASIS] + sums[BASIS : 2 * BASIS]) / sums[2 * BASIS : 2 * BASIS + 1]
        for k in range(packed):
            pieces[start + k][f] = mean[:, k * places : (k + 1) * places]
    own = jnp.concatenate([query_lanes(received), ones[:, :tokens]], axis=0)
    combined = jnp.concatenate(
        [own]
        + [cat(piece, 1) for piece in pieces]
        + [jnp.zeros((depth - used, tokens), F32)]
        + [query_lanes(received, k) for k in (1, 2)],
        axis=0,
    ).astype(BF16)
    combined = dot(combined, order)
    noise = combined[depth : depth + channels] + combined[depth + channels :]
    combined = combined[:depth]

    stream = dot(mixt_ref[...], combined.astype(BF16))
    stream_ref[...] = stream
    variance = jnp.mean(stream * stream, axis=0, keepdims=True)
    placed = (iota((depth - used, tokens), 1) & (plan.low - 1)) == iota((depth - used, tokens), 0)
    combined = jnp.concatenate(
        [combined[:used] * lax.rsqrt(variance + EPS), placed.astype(F32)], axis=0
    ).astype(BF16)
    keys = dot(combined, key_ref[...], 0, 0).astype(BF16)
    queries = dot(query_ref[...], combined).astype(BF16)
    units = [(slice(g, g + LANES), h) for g in range(0, tokens, LANES) for h in range(HEADS)]
    scores = [
        dot(
            keys[cut, h * LANES : h * LANES + plan.qpad],
            queries[h * plan.qpad : (h + 1) * plan.qpad, cut],
        )
        for cut, h in units
    ]
    values = dot(value_ref[...], combined).astype(BF16)
    weights, totals = [], []
    for score in scores:
        weight = jnp.exp2(score - jnp.max(score, axis=0, keepdims=True))
        totals.append(jnp.sum(weight, axis=0, keepdims=True))
        weights.append(weight.astype(BF16))
    for (cut, h), weight, total in zip(units, weights, totals):
        mean = dot(values[h * VPAD : (h + 1) * VPAD, cut], weight) / total
        mixed_ref[pl.ds(h * HEAD_DIM, HEAD_DIM), cut] = mean[:HEAD_DIM]

    outt_copy.wait()
    delta = dot(outt_ref[...], mixed_ref[...].astype(BF16))
    average = delta[:1] + delta[1:2]
    stream = (stream_ref[...] - average) + delta[16:]
    variance = jnp.mean(stream * stream, axis=0, keepdims=True)
    predicted = dot(finalt_ref[...], stream.astype(BF16)) * lax.rsqrt(variance + EPS)
    gap = predicted - noise
    errors = jnp.mean(gap * gap, axis=0, keepdims=True)
    high, rest = split(errors)
    middle, rest = split(rest)
    parts = jnp.concatenate([high, middle, rest] + [jnp.zeros_like(rest)] * 5, axis=0)
    errors = jnp.sum(dot(parts.astype(BF16), order, 1, 1), axis=0, keepdims=True)
    lanes = out_ref.shape[1]
    for k in range(tokens // lanes):
        out_ref[pl.ds(k, 1), :] = errors[:, k * lanes : (k + 1) * lanes]


def grant(mib):
    return pltpu.CompilerParams(vmem_limit_bytes=mib << 20)


def near(value):
    return pltpu.with_memory_space_constraint(value, pltpu.VMEM)


def far(value):
    return pltpu.with_memory_space_constraint(value, pltpu.HBM)


def local(
    latents,
    target_noise,
    timesteps,
    patch_weight,
    time_weight,
    spatial_project,
    spatial_output,
    temporal_project,
    temporal_output,
    final_weight,
):
    videos, _, rows, cols, channels = latents.shape
    frames, halves = lax.axis_size("frame"), lax.axis_size("row")
    plan = Plan(videos, rows, cols, frames, halves)
    inner, model = spatial_output.shape
    depth = -(-(HEADS + 1) * BASIS // LANES) * LANES
    shape = jax.ShapeDtypeStruct

    def by_row(value):
        return value.reshape(videos, rows, cols, channels).transpose(0, 1, 3, 2)

    send, time_near = pl.pallas_call(
        functools.partial(pack_kernel, plan),
        out_shape=(
            pltpu.VMEM((frames * halves, channels, plan.width), BF16),
            pltpu.VMEM(time_weight.shape, time_weight.dtype),
        ),
        in_specs=[HBM] * 4,
        out_specs=(VMEM,) * 2,
        compiler_params=grant(26),
        scratch_shapes=[
            pltpu.SMEM(timesteps.shape, timesteps.dtype),
            pltpu.VMEM((videos, rows, channels, cols), F32),
            pltpu.VMEM((videos, rows, channels, cols), F32),
            pltpu.SemaphoreType.DMA((4,)),
        ],
    )(*map(far, (timesteps, by_row(latents), by_row(target_noise), time_weight)))
    received = lax.all_to_all(send, ("frame", "row"), 0, 0, tiled=True)

    weights = (
        patch_weight,
        spatial_project.T,
        spatial_output,
        temporal_project.T,
        temporal_output,
    )
    tables = pl.pallas_call(
        functools.partial(fold_kernel, plan),
        out_shape=(
            pltpu.VMEM((3 * BASIS, BASIS), BF16),
            pltpu.VMEM((HEADS * BASIS, 3 * BASIS), BF16),
            pltpu.VMEM((model, depth), BF16),
            pltpu.VMEM((HEADS * plan.qpad, depth), BF16),
            pltpu.VMEM((depth, HEADS * LANES), BF16),
            pltpu.VMEM((HEADS * VPAD, depth), BF16),
            pltpu.HBM((model + 16, inner), BF16),
            pltpu.VMEM((plan.tokens + plan.places - plan.low, LANES), BF16),
            pltpu.VMEM((plan.marks, LANES), F32),
        ),
        in_specs=[VMEM] + [HBM] * (1 + len(weights)),
        out_specs=(VMEM,) * 6 + (HBM,) + (VMEM,) * 2,
        scratch_shapes=[pltpu.SMEM(timesteps.shape, timesteps.dtype)]
        + [pltpu.VMEM(w.shape, w.dtype) for w in weights]
        + [pltpu.VMEM((model + 16, inner), BF16), pltpu.SemaphoreType.DMA((11,))],
        compiler_params=grant(26),
    )(near(time_near), *map(far, (timesteps, *weights)))

    outt = tables[6]
    lanes = min(plan.places, cols)
    errors = pl.pallas_call(
        functools.partial(main_kernel, plan),
        out_shape=shape((plan.tokens // lanes, lanes), F32),
        in_specs=[VMEM] * 7 + [HBM] + [VMEM] * 3,
        out_specs=VMEM,
        compiler_params=grant(26),
        scratch_shapes=[
            pltpu.VMEM((inner, plan.tokens), F32),
            pltpu.VMEM((model, plan.tokens), F32),
            pltpu.VMEM(outt.shape, outt.dtype),
            pltpu.VMEM((frames, channels, plan.width), F32),
            pltpu.SemaphoreType.DMA,
        ],
    )(
        *map(near, (received, *tables[:6])),
        far(outt),
        *map(near, (*tables[7:], final_weight.T)),
    )
    errors = lax.all_to_all(errors, "frame", 0, 0, tiled=True)
    return errors.reshape(videos, 1, rows, cols)


def solution(mesh):
    return jax.shard_map(
        local,
        mesh=mesh,
        in_specs=(
            P("grp", "frame", "row", None, None),
            P("grp", "frame", "row", None, None),
            P("grp"),
            P(),
            P(),
            P(),
            P(),
            P(),
            P(),
            P(),
        ),
        out_specs=P("grp", "frame", "row", None),
        check_vma=False,
    )
```

```python
import functools
import math

import jax
import jax.numpy as jnp
from jax import lax
from jax.experimental import pallas as pl
from jax.experimental.pallas import tpu as pltpu
from jax.sharding import PartitionSpec as P

HEAD_DIM = 72
HEADS = 8
STEPS = 1000
REACH = 2
EPS = 1e-06
LANES = 128
BASIS = 24
VPAD = 80
F32 = jnp.float32
BF16 = jnp.bfloat16
VMEM = pl.BlockSpec(memory_space=pltpu.VMEM)
SMEM = pl.BlockSpec(memory_space=pltpu.SMEM)
HBM = pl.BlockSpec(memory_space=pltpu.HBM)


def dot(a, b, ca=1, cb=0, precision=None):
    return lax.dot_general(
        a, b, (((ca,), (cb,)), ((), ())), preferred_element_type=F32, precision=precision
    )


def split(x):
    high = x.astype(BF16).astype(F32)
    return high, x - high


def iota(shape, dim):
    return lax.broadcasted_iota(jnp.int32, shape, dim)


def cat(parts, axis):
    return parts[0] if len(parts) == 1 else jnp.concatenate(parts, axis=axis)


class Plan:
    def __init__(self, videos, rows, cols, frames, halves):
        self.videos, self.rows, self.cols = videos, rows, cols
        self.frames, self.halves = frames, halves
        self.chunks = frames // videos
        self.places = rows * cols // self.chunks
        self.qrows = max(1, self.places // cols)
        self.window = (self.qrows + 2 * REACH) * cols
        self.width = -(-(self.window + 3 * self.places) // LANES) * LANES
        self.tokens = frames * self.places
        self.low = LANES // frames
        self.stride = -(-(self.window + self.places) // LANES) * LANES
        self.marks = -(-(self.qrows + 2 * REACH) // 8) * 8
        self.qpad = -(-(HEAD_DIM + self.low) // 16) * 16
        whole = self.qrows * cols if self.places >= cols else cols
        assert frames % videos == 0 and (rows * cols) % self.chunks == 0
        assert self.places % cols == 0 or cols % self.places == 0
        assert rows >= REACH and rows % self.qrows == 0 and whole >= self.places
        for size in (cols, frames, self.places, self.low):
            assert size & (size - 1) == 0 and size > 0
        assert self.places % self.low == 0 and self.tokens % LANES == 0


def log_kept(step):
    counter = iota((8, LANES), 0) * LANES + iota((8, LANES), 1)
    beta = 0.0001 + (0.02 - 0.0001) * counter.astype(F32) / (STEPS - 1)
    used = (counter <= step) & (counter < STEPS)
    terms = jnp.where(used, jnp.log1p(-jnp.where(used, beta, 0.0)), 0.0)
    return jnp.sum(jnp.sum(terms, axis=0, keepdims=True), axis=1, keepdims=True)


def pack_kernel(
    plan,
    steps_hbm,
    latents_hbm,
    noise_hbm,
    time_hbm,
    send_ref,
    time_ref,
    steps_ref,
    latents_ref,
    noise_ref,
    sems,
):
    pairs = [(steps_hbm, steps_ref), (latents_hbm, latents_ref), (noise_hbm, noise_ref)]
    pairs += [(time_hbm, time_ref)]
    copies = [
        pltpu.make_async_copy(source, target, sems.at[k])
        for k, (source, target) in enumerate(pairs)
    ]
    for copy in copies:
        copy.start()
    for copy in copies[:3]:
        copy.wait()
    half = lax.axis_index("row")
    channels = latents_ref.shape[2]
    videos = []
    for video in range(plan.videos):
        kept = jnp.exp(log_kept(steps_ref[video]))
        signal, spread = jnp.sqrt(kept), jnp.sqrt(1.0 - kept)
        noise = cat([noise_ref[video, row] for row in range(plan.rows)], 1)
        clean = cat([latents_ref[video, row] for row in range(plan.rows)], 1)
        videos.append((signal * clean + spread * noise, *split(noise)))

    def window(value, start, count):
        first, last = max(start, 0), min(start + count, plan.rows)
        if first >= last:
            return jnp.zeros((channels, count * plan.cols), F32)
        parts = []
        if first > start:
            parts.append(jnp.zeros((channels, (first - start) * plan.cols), F32))
        parts.append(value[:, first * plan.cols : last * plan.cols])
        if last < start + count:
            parts.append(jnp.zeros((channels, (start + count - last) * plan.cols), F32))
        return cat(parts, 1)

    unused = plan.width - plan.window - 3 * plan.places
    for target in range(plan.halves):
        for apart in range(1 - plan.halves, plan.halves):
            if not 0 <= target + apart < plan.halves:
                continue

            @pl.when(half == target + apart)
            def _():
                for peer in range(plan.frames):
                    values = videos[peer // plan.chunks]
                    place = (peer % plan.chunks) * plan.places
                    start = place // plan.cols - REACH - apart * plan.rows
                    parts = [window(values[0], start, plan.qrows + 2 * REACH)]
                    if apart == 0:
                        parts += [v[:, place : place + plan.places] for v in values]
                        if unused:
                            parts.append(jnp.zeros((channels, unused), F32))
                    else:
                        parts.append(jnp.zeros((channels, plan.width - plan.window), F32))
                    send_ref[peer * plan.halves + target] = cat(parts, 1).astype(BF16)
    copies[3].wait()


def fold_kernel(
    plan,
    time_ref,
    steps_hbm,
    patch_hbm,
    sproject_hbm,
    soutput_hbm,
    tproject_hbm,
    toutput_hbm,
    gram_ref,
    score_ref,
    mixt_ref,
    query_ref,
    key_ref,
    value_ref,
    outt_hbm,
    order_ref,
    rows_ref,
    steps_ref,
    patch_ref,
    sproject_ref,
    soutput_ref,
    tproject_ref,
    toutput_ref,
    outt_ref,
    sems,
):
    model = patch_ref.shape[1]
    inner = soutput_ref.shape[0]
    halfway = time_ref.shape[0] // 2
    tokens, places, low = plan.tokens, plan.places, plan.low
    scale = math.log2(math.e) / math.sqrt(HEAD_DIM)
    parts = [slice(k * inner, (k + 1) * inner) for k in range(3)]
    pairs = [(steps_hbm, steps_ref), (patch_hbm, patch_ref), (toutput_hbm, toutput_ref)]
    pairs += [(sproject_hbm.at[cut], sproject_ref.at[cut]) for cut in parts]
    pairs += [(soutput_hbm, soutput_ref)]
    pairs += [(tproject_hbm.at[cut], tproject_ref.at[cut]) for cut in parts]
    copies = [
        pltpu.make_async_copy(source, target, sems.at[k])
        for k, (source, target) in enumerate(pairs)
    ]
    for copy in copies:
        copy.start()

    lane = iota(order_ref.shape, 1)
    row = iota(order_ref.shape, 0) - (places // low - 1) * low
    order_ref[...] = (row == (lane // low) * places + (lane & (low - 1))).astype(BF16)

    half = lax.axis_index("row")
    chunk = lax.rem(lax.axis_index("frame"), plan.chunks)
    top = half * plan.rows + lax.div(chunk * places, plan.cols) - REACH
    key_row = iota((plan.marks, LANES), 0)
    query = iota((plan.marks, LANES), 1) & (places - 1)
    query_row = jnp.zeros((plan.marks, LANES), jnp.int32)
    for k in range(1, plan.qrows):
        query_row = query_row + (query >= k * plan.cols).astype(jnp.int32)
    seen = (key_row >= query_row) & (key_row <= query_row + 2 * REACH)
    seen = seen & (key_row + top >= 0) & (key_row + top < plan.halves * plan.rows)
    rows_ref[...] = jnp.where(seen, 0.0, -1e30)

    copies[0].wait()
    step = steps_ref[lax.axis_index("frame") // plan.chunks]
    freqs = jnp.exp(iota((8, halfway), 1).astype(F32) * (-math.log(10000.0) / halfway))
    angles = step.astype(F32) * freqs
    features = jnp.concatenate([jnp.cos(angles), jnp.sin(angles)], axis=1).astype(BF16)
    time_vector = dot(features, time_ref[...])
    time_rows = jnp.where(iota((8, model), 0) == 0, time_vector, 0.0)
    copies[1].wait()
    basis = jnp.concatenate([patch_ref[...].astype(F32), time_rows], axis=0)
    basis = basis - jnp.mean(basis, axis=1, keepdims=True)

    gram = dot(basis, basis, 1, 1, lax.Precision.HIGHEST) * (1.0 / model)
    high, rest = split(gram)
    middle, rest = split(rest)
    gram_ref[...] = jnp.concatenate([high, middle, rest], axis=0).astype(BF16)

    copies[2].wait()
    average = dot(jnp.ones((8, model), BF16), toutput_ref[...], 1, 1)[:1] * (1.0 / model)
    high, rest = split(average)
    outt_ref[pl.ds(16, model), :] = toutput_ref[...].T
    outt_ref[pl.ds(0, 16), :] = jnp.concatenate(
        [high, rest, jnp.zeros((14, inner), F32)], axis=0
    ).astype(BF16)
    outt_copy = pltpu.make_async_copy(outt_ref, outt_hbm, sems.at[10])
    outt_copy.start()

    both = jnp.concatenate(split(basis), axis=0).astype(BF16)
    folded = []
    for k in range(3):
        copies[3 + k].wait()
        if k == 2:
            copies[6].wait()
        value = dot(both, sproject_ref[parts[k], :], 1, 1)
        folded.append(value[:BASIS] + value[BASIS:])
    queries, keys, values = folded
    def by_head(value, first, count):
        lane = iota(value.shape, 1)
        return [
            jnp.where((lane >= h * HEAD_DIM) & (lane < (h + 1) * HEAD_DIM), value, 0.0)
            for h in range(first, first + count)
        ]

    khigh, krest = (
        jnp.concatenate(by_head(v, 0, HEADS), axis=0).astype(BF16) for v in split(keys)
    )
    qhigh, qrest = split(queries * scale)
    both = dot(jnp.concatenate([qhigh, qrest], axis=0).astype(BF16), khigh, 1, 1)
    score = both[:BASIS] + both[BASIS:] + dot(qhigh.astype(BF16), krest, 1, 1)
    unused = jnp.zeros((LANES - BASIS, HEADS * BASIS), F32)
    high, rest = split(jnp.concatenate([score, unused], axis=0).T[:, :BASIS])
    score_ref[...] = jnp.concatenate([high, high, rest], axis=1).astype(BF16)

    group = 2 if (2 * HEAD_DIM) % 16 == 0 else HEADS
    mixed = []
    for first in range(0, HEADS, group):
        cut = slice(first * HEAD_DIM, (first + group) * HEAD_DIM)
        both = jnp.concatenate(
            [part for v in split(values[:, cut]) for part in by_head(v, 0, group)], axis=0
        )
        both = dot(both.astype(BF16), soutput_ref[cut, :])
        mixed.append(both[: group * BASIS] + both[group * BASIS :])
    mixed = jnp.concatenate(mixed, axis=0)
    mixed = mixed - jnp.mean(mixed, axis=1, keepdims=True)
    depth = mixt_ref.shape[1]
    used = (HEADS + 1) * BASIS
    whole = jnp.concatenate([basis, mixed, jnp.zeros((depth - used, model), F32)], axis=0)
    whole = whole.astype(BF16)
    mixt_ref[...] = whole.T

    for copy in copies[7:]:
        copy.wait()
    folded = []
    for k in range(3):
        folded.append(dot(tproject_ref[parts[k], :], whole, 1, 1))
    queries, keys, values = folded
    mark = iota((LANES - HEAD_DIM, depth), 1) - used
    row = iota((LANES - HEAD_DIM, depth), 0)
    placed = (mark >= 0) & (mark < low) & (row < low)
    key_mark = jnp.where(placed & (mark == row), 1.0, 0.0)
    query_mark = jnp.where(placed & (mark != row), -1e30, 0.0)[: plan.qpad - HEAD_DIM]
    blank = jnp.zeros((VPAD - HEAD_DIM, depth), F32)
    padded = []
    for h in range(HEADS):
        cut = slice(h * HEAD_DIM, (h + 1) * HEAD_DIM)
        padded += [keys[cut], key_mark]
        query_ref[pl.ds(h * plan.qpad, plan.qpad), :] = jnp.concatenate(
            [queries[cut] * scale, query_mark], axis=0
        ).astype(BF16)
        value_ref[pl.ds(h * VPAD, VPAD), :] = jnp.concatenate(
            [values[cut], blank], axis=0
        ).astype(BF16)
    key_ref[...] = jnp.concatenate(padded, axis=0).astype(BF16).T
    outt_copy.wait()


def main_kernel(
    plan,
    recv_ref,
    gram_ref,
    score_ref,
    mixt_ref,
    query_ref,
    key_ref,
    value_ref,
    outt_hbm,
    order_ref,
    rows_ref,
    finalt_ref,
    out_ref,
    mixed_ref,
    stream_ref,
    outt_ref,
    total_ref,
    sem,
):
    window, places, tokens = plan.window, plan.places, plan.tokens
    frames, stride = plan.frames, plan.stride
    channels = recv_ref.shape[1]
    depth = mixt_ref.shape[1]
    used = (HEADS + 1) * BASIS

    outt_copy = pltpu.make_async_copy(outt_hbm, outt_ref, sem)
    outt_copy.start()
    groups = range(places // plan.low)
    order = cat(
        [order_ref[pl.ds((len(groups) - 1 - k) * plan.low, tokens), :] for k in groups], 1
    )

    def add(f, carry):
        value = recv_ref[f * plan.halves].astype(F32)
        for r in range(1, plan.halves):
            value = value + recv_ref[f * plan.halves + r].astype(F32)
        total_ref[f] = value
        return carry

    lax.fori_loop(0, frames, add, 0)
    received = [total_ref[f] for f in range(frames)]

    def query_lanes(values, k=0):
        return cat([v[:, window + k * places : window + (k + 1) * places] for v in values], 1)

    ones = (iota((BASIS - channels, frames * stride), 0) == 0).astype(F32)
    basis = jnp.concatenate([cat([v[:, :stride] for v in received], 1), ones], axis=0)
    image = dot(gram_ref[...], basis.astype(BF16))
    image = image[:BASIS] + image[BASIS : 2 * BASIS] + image[2 * BASIS :]
    variance = jnp.sum(basis * image, axis=0, keepdims=True)
    scaled = basis * lax.rsqrt(jnp.maximum(variance, 0.0) + EPS)
    high, rest = split(scaled)
    by_frame = [slice(f * stride, (f + 1) * stride) for f in range(frames)]
    qhigh, qrest = (query_lanes([v[:, cut] for cut in by_frame]) for v in (high, rest))
    turned = dot(score_ref[...], jnp.concatenate([qhigh, qrest, qhigh], axis=0).astype(BF16))
    qhigh, qrest = split(turned)

    packed = min(HEADS, 2 * LANES // places)
    sides = cat([rows_ref[...]] * (packed * places // LANES), 1)
    starts = range(0, HEADS, packed)
    key_row = jnp.zeros((plan.marks, stride), jnp.int32)
    for k in range(1, window // plan.cols):
        key_row = key_row + (iota((plan.marks, stride), 1) >= k * plan.cols).astype(jnp.int32)
    marks = (iota((plan.marks, stride), 0) == key_row).astype(F32)
    count = (iota((8, window), 0) == 0).astype(F32)

    def gather(value, f, start):
        return cat(
            [
                value[h * BASIS : (h + 1) * BASIS, f * places : (f + 1) * places]
                for h in range(start, start + packed)
            ],
            1,
        )

    scores, lefts = [], []
    for f in range(frames):
        fhigh, frest = high[:, by_frame[f]], rest[:, by_frame[f]]
        left = jnp.concatenate([fhigh, fhigh, frest, marks], axis=0).T.astype(BF16)[:window]
        lefts.append(
            jnp.concatenate([fhigh[:, :window], frest[:, :window], count], axis=0).astype(BF16)
        )
        for start in starts:
            ahigh, arest = gather(qhigh, f, start), gather(qrest, f, start)
            right = jnp.concatenate([ahigh, arest, ahigh, sides], axis=0)
            scores.append(dot(left, right.astype(BF16)))
    weights = [
        jnp.exp2(score - jnp.max(score, axis=0, keepdims=True)).astype(BF16)
        for score in scores
    ]
    pieces = [[None] * frames for _ in range(HEADS)]
    for n, weight in enumerate(weights):
        f, start = n // len(starts), (n % len(starts)) * packed
        sums = dot(lefts[f], weight)
        mean = (sums[:BASIS] + sums[BASIS : 2 * BASIS]) / sums[2 * BASIS : 2 * BASIS + 1]
        for k in range(packed):
            pieces[start + k][f] = mean[:, k * places : (k + 1) * places]
    own = jnp.concatenate([query_lanes(received), ones[:, :tokens]], axis=0)
    combined = jnp.concatenate(
        [own]
        + [cat(piece, 1) for piece in pieces]
        + [jnp.zeros((depth - used, tokens), F32)]
        + [query_lanes(received, k) for k in (1, 2)],
        axis=0,
    ).astype(BF16)
    combined = dot(combined, order)
    noise = combined[depth : depth + channels] + combined[depth + channels :]
    combined = combined[:depth]

    stream = dot(mixt_ref[...], combined.astype(BF16))
    stream_ref[...] = stream
    variance = jnp.mean(stream * stream, axis=0, keepdims=True)
    placed = (iota((depth - used, tokens), 1) & (plan.low - 1)) == iota((depth - used, tokens), 0)
    combined = jnp.concatenate(
        [combined[:used] * lax.rsqrt(variance + EPS), placed.astype(F32)], axis=0
    ).astype(BF16)
    keys = dot(combined, key_ref[...], 0, 0).astype(BF16)
    queries = dot(query_ref[...], combined).astype(BF16)
    units = [(slice(g, g + LANES), h) for g in range(0, tokens, LANES) for h in range(HEADS)]
    scores = [
        dot(
            keys[cut, h * LANES : h * LANES + plan.qpad],
            queries[h * plan.qpad : (h + 1) * plan.qpad, cut],
        )
        for cut, h in units
    ]
    values = dot(value_ref[...], combined).astype(BF16)
    weights, totals = [], []
    for score in scores:
        weight = jnp.exp2(score - jnp.max(score, axis=0, keepdims=True))
        totals.append(jnp.sum(weight, axis=0, keepdims=True))
        weights.append(weight.astype(BF16))
    for (cut, h), weight, total in zip(units, weights, totals):
        mean = dot(values[h * VPAD : (h + 1) * VPAD, cut], weight) / total
        mixed_ref[pl.ds(h * HEAD_DIM, HEAD_DIM), cut] = mean[:HEAD_DIM]

    outt_copy.wait()
    delta = dot(outt_ref[...], mixed_ref[...].astype(BF16))
    average = delta[:1] + delta[1:2]
    stream = (stream_ref[...] - average) + delta[16:]
    variance = jnp.mean(stream * stream, axis=0, keepdims=True)
    predicted = dot(finalt_ref[...], stream.astype(BF16)) * lax.rsqrt(variance + EPS)
    gap = predicted - noise
    errors = jnp.mean(gap * gap, axis=0, keepdims=True)
    high, rest = split(errors)
    middle, rest = split(rest)
    parts = jnp.concatenate([high, middle, rest] + [jnp.zeros_like(rest)] * 5, axis=0)
    errors = jnp.sum(dot(parts.astype(BF16), order, 1, 1), axis=0, keepdims=True)
    lanes = out_ref.shape[1]
    for k in range(tokens // lanes):
        out_ref[pl.ds(k, 1), :] = errors[:, k * lanes : (k + 1) * lanes]


def grant(mib):
    return pltpu.CompilerParams(vmem_limit_bytes=mib << 20)


def near(value):
    return pltpu.with_memory_space_constraint(value, pltpu.VMEM)


def far(value):
    return pltpu.with_memory_space_constraint(value, pltpu.HBM)


def local(
    latents,
    target_noise,
    timesteps,
    patch_weight,
    time_weight,
    spatial_project,
    spatial_output,
    temporal_project,
    temporal_output,
    final_weight,
):
    videos, _, rows, cols, channels = latents.shape
    frames, halves = lax.axis_size("frame"), lax.axis_size("row")
    plan = Plan(videos, rows, cols, frames, halves)
    inner, model = spatial_output.shape
    depth = -(-(HEADS + 1) * BASIS // LANES) * LANES
    shape = jax.ShapeDtypeStruct

    def by_row(value):
        return value.reshape(videos, rows, cols, channels).transpose(0, 1, 3, 2)

    send, time_near = pl.pallas_call(
        functools.partial(pack_kernel, plan),
        out_shape=(
            pltpu.VMEM((frames * halves, channels, plan.width), BF16),
            pltpu.VMEM(time_weight.shape, time_weight.dtype),
        ),
        in_specs=[HBM] * 4,
        out_specs=(VMEM,) * 2,
        compiler_params=grant(26),
        scratch_shapes=[
            pltpu.SMEM(timesteps.shape, timesteps.dtype),
            pltpu.VMEM((videos, rows, channels, cols), F32),
            pltpu.VMEM((videos, rows, channels, cols), F32),
            pltpu.SemaphoreType.DMA((4,)),
        ],
    )(*map(far, (timesteps, by_row(latents), by_row(target_noise), time_weight)))
    received = lax.all_to_all(send, ("frame", "row"), 0, 0, tiled=True)

    weights = (
        patch_weight,
        spatial_project.T,
        spatial_output,
        temporal_project.T,
        temporal_output,
    )
    tables = pl.pallas_call(
        functools.partial(fold_kernel, plan),
        out_shape=(
            pltpu.VMEM((3 * BASIS, BASIS), BF16),
            pltpu.VMEM((HEADS * BASIS, 3 * BASIS), BF16),
            pltpu.VMEM((model, depth), BF16),
            pltpu.VMEM((HEADS * plan.qpad, depth), BF16),
            pltpu.VMEM((depth, HEADS * LANES), BF16),
            pltpu.VMEM((HEADS * VPAD, depth), BF16),
            pltpu.HBM((model + 16, inner), BF16),
            pltpu.VMEM((plan.tokens + plan.places - plan.low, LANES), BF16),
            pltpu.VMEM((plan.marks, LANES), F32),
        ),
        in_specs=[VMEM] + [HBM] * (1 + len(weights)),
        out_specs=(VMEM,) * 6 + (HBM,) + (VMEM,) * 2,
        scratch_shapes=[pltpu.SMEM(timesteps.shape, timesteps.dtype)]
        + [pltpu.VMEM(w.shape, w.dtype) for w in weights]
        + [pltpu.VMEM((model + 16, inner), BF16), pltpu.SemaphoreType.DMA((11,))],
        compiler_params=grant(26),
    )(near(time_near), *map(far, (timesteps, *weights)))

    outt = tables[6]
    lanes = min(plan.places, cols)
    errors = pl.pallas_call(
        functools.partial(main_kernel, plan),
        out_shape=shape((plan.tokens // lanes, lanes), F32),
        in_specs=[VMEM] * 7 + [HBM] + [VMEM] * 3,
        out_specs=VMEM,
        compiler_params=grant(26),
        scratch_shapes=[
            pltpu.VMEM((inner, plan.tokens), F32),
            pltpu.VMEM((model, plan.tokens), F32),
            pltpu.VMEM(outt.shape, outt.dtype),
            pltpu.VMEM((frames, channels, plan.width), F32),
            pltpu.SemaphoreType.DMA,
        ],
    )(
        *map(near, (received, *tables[:6])),
        far(outt),
        *map(near, (*tables[7:], final_weight.T)),
    )
    errors = lax.all_to_all(errors, "frame", 0, 0, tiled=True)
    return errors.reshape(videos, 1, rows, cols)


def solution(mesh):
    return jax.shard_map(
        local,
        mesh=mesh,
        in_specs=(
            P("grp", "frame", "row", None, None),
            P("grp", "frame", "row", None, None),
            P("grp"),
            P(),
            P(),
            P(),
            P(),
            P(),
            P(),
            P(),
        ),
        out_specs=P("grp", "frame", "row", None),
        check_vma=False,
    )
```

```python
import functools
import math

import jax
import jax.numpy as jnp
from jax import lax
from jax.experimental import pallas as pl
from jax.experimental.pallas import tpu as pltpu
from jax.sharding import PartitionSpec as P

HEAD_DIM = 72
HEADS = 8
STEPS = 1000
REACH = 2
EPS = 1e-06
LANES = 128
BASIS = 24
VPAD = 80
F32 = jnp.float32
BF16 = jnp.bfloat16
VMEM = pl.BlockSpec(memory_space=pltpu.VMEM)
SMEM = pl.BlockSpec(memory_space=pltpu.SMEM)
HBM = pl.BlockSpec(memory_space=pltpu.HBM)


def dot(a, b, ca=1, cb=0, precision=None):
    return lax.dot_general(
        a, b, (((ca,), (cb,)), ((), ())), preferred_element_type=F32, precision=precision
    )


def split(x):
    high = x.astype(BF16).astype(F32)
    return high, x - high


def iota(shape, dim):
    return lax.broadcasted_iota(jnp.int32, shape, dim)


def cat(parts, axis):
    return parts[0] if len(parts) == 1 else jnp.concatenate(parts, axis=axis)


class Plan:
    def __init__(self, videos, rows, cols, frames, halves):
        self.videos, self.rows, self.cols = videos, rows, cols
        self.frames, self.halves = frames, halves
        self.chunks = frames // videos
        self.places = rows * cols // self.chunks
        self.qrows = max(1, self.places // cols)
        self.window = (self.qrows + 2 * REACH) * cols
        self.width = -(-(self.window + 3 * self.places) // LANES) * LANES
        self.tokens = frames * self.places
        self.low = LANES // frames
        self.stride = -(-(self.window + self.places) // LANES) * LANES
        self.marks = -(-(self.qrows + 2 * REACH) // 8) * 8
        self.qpad = -(-(HEAD_DIM + self.low) // 16) * 16
        whole = self.qrows * cols if self.places >= cols else cols
        assert frames % videos == 0 and (rows * cols) % self.chunks == 0
        assert self.places % cols == 0 or cols % self.places == 0
        assert rows >= REACH and rows % self.qrows == 0 and whole >= self.places
        for size in (cols, frames, self.places, self.low):
            assert size & (size - 1) == 0 and size > 0
        assert self.places % self.low == 0 and self.tokens % LANES == 0


def log_kept(step):
    counter = iota((8, LANES), 0) * LANES + iota((8, LANES), 1)
    beta = 0.0001 + (0.02 - 0.0001) * counter.astype(F32) / (STEPS - 1)
    used = (counter <= step) & (counter < STEPS)
    terms = jnp.where(used, jnp.log1p(-jnp.where(used, beta, 0.0)), 0.0)
    return jnp.sum(jnp.sum(terms, axis=0, keepdims=True), axis=1, keepdims=True)


def pack_kernel(
    plan,
    steps_hbm,
    latents_hbm,
    noise_hbm,
    time_hbm,
    send_ref,
    time_ref,
    steps_ref,
    latents_ref,
    noise_ref,
    sems,
):
    pairs = [(steps_hbm, steps_ref), (latents_hbm, latents_ref), (noise_hbm, noise_ref)]
    pairs += [(time_hbm, time_ref)]
    copies = [
        pltpu.make_async_copy(source, target, sems.at[k])
        for k, (source, target) in enumerate(pairs)
    ]
    for copy in copies:
        copy.start()
    for copy in copies[:3]:
        copy.wait()
    half = lax.axis_index("row")
    channels = latents_ref.shape[2]
    videos = []
    for video in range(plan.videos):
        kept = jnp.exp(log_kept(steps_ref[video]))
        signal, spread = jnp.sqrt(kept), jnp.sqrt(1.0 - kept)
        noise = cat([noise_ref[video, row] for row in range(plan.rows)], 1)
        clean = cat([latents_ref[video, row] for row in range(plan.rows)], 1)
        videos.append((signal * clean + spread * noise, *split(noise)))

    def window(value, start, count):
        first, last = max(start, 0), min(start + count, plan.rows)
        if first >= last:
            return jnp.zeros((channels, count * plan.cols), F32)
        parts = []
        if first > start:
            parts.append(jnp.zeros((channels, (first - start) * plan.cols), F32))
        parts.append(value[:, first * plan.cols : last * plan.cols])
        if last < start + count:
            parts.append(jnp.zeros((channels, (start + count - last) * plan.cols), F32))
        return cat(parts, 1)

    unused = plan.width - plan.window - 3 * plan.places
    for target in range(plan.halves):
        for apart in range(1 - plan.halves, plan.halves):
            if not 0 <= target + apart < plan.halves:
                continue

            @pl.when(half == target + apart)
            def _():
                for peer in range(plan.frames):
                    values = videos[peer // plan.chunks]
                    place = (peer % plan.chunks) * plan.places
                    start = place // plan.cols - REACH - apart * plan.rows
                    parts = [window(values[0], start, plan.qrows + 2 * REACH)]
                    if apart == 0:
                        parts += [v[:, place : place + plan.places] for v in values]
                        if unused:
                            parts.append(jnp.zeros((channels, unused), F32))
                    else:
                        parts.append(jnp.zeros((channels, plan.width - plan.window), F32))
                    send_ref[peer * plan.halves + target] = cat(parts, 1).astype(BF16)
    copies[3].wait()


def fold_kernel(
    plan,
    time_ref,
    steps_hbm,
    patch_hbm,
    sproject_hbm,
    soutput_hbm,
    tproject_hbm,
    toutput_hbm,
    gram_ref,
    score_ref,
    mixt_ref,
    query_ref,
    key_ref,
    value_ref,
    outt_hbm,
    order_ref,
    rows_ref,
    steps_ref,
    patch_ref,
    sproject_ref,
    soutput_ref,
    tproject_ref,
    toutput_ref,
    outt_ref,
    sems,
):
    model = patch_ref.shape[1]
    inner = soutput_ref.shape[0]
    halfway = time_ref.shape[0] // 2
    tokens, places, low = plan.tokens, plan.places, plan.low
    scale = math.log2(math.e) / math.sqrt(HEAD_DIM)
    parts = [slice(k * inner, (k + 1) * inner) for k in range(3)]
    pairs = [(steps_hbm, steps_ref), (patch_hbm, patch_ref), (toutput_hbm, toutput_ref)]
    pairs += [(sproject_hbm.at[cut], sproject_ref.at[cut]) for cut in parts]
    pairs += [(soutput_hbm, soutput_ref)]
    total = 3 * inner
    halves = [slice(0, total // 2), slice(total // 2, total)]
    pairs += [(tproject_hbm.at[cut], tproject_ref.at[cut]) for cut in halves]
    copies = [
        pltpu.make_async_copy(source, target, sems.at[k])
        for k, (source, target) in enumerate(pairs)
    ]
    for copy in copies:
        copy.start()

    lane = iota(order_ref.shape, 1)
    row = iota(order_ref.shape, 0) - (places // low - 1) * low
    order_ref[...] = (row == (lane // low) * places + (lane & (low - 1))).astype(BF16)

    half = lax.axis_index("row")
    chunk = lax.rem(lax.axis_index("frame"), plan.chunks)
    top = half * plan.rows + lax.div(chunk * places, plan.cols) - REACH
    key_row = iota((plan.marks, LANES), 0)
    query = iota((plan.marks, LANES), 1) & (places - 1)
    query_row = jnp.zeros((plan.marks, LANES), jnp.int32)
    for k in range(1, plan.qrows):
        query_row = query_row + (query >= k * plan.cols).astype(jnp.int32)
    seen = (key_row >= query_row) & (key_row <= query_row + 2 * REACH)
    seen = seen & (key_row + top >= 0) & (key_row + top < plan.halves * plan.rows)
    rows_ref[...] = jnp.where(seen, 0.0, -1e30)

    copies[0].wait()
    step = steps_ref[lax.axis_index("frame") // plan.chunks]
    freqs = jnp.exp(iota((8, halfway), 1).astype(F32) * (-math.log(10000.0) / halfway))
    angles = step.astype(F32) * freqs
    features = jnp.concatenate([jnp.cos(angles), jnp.sin(angles)], axis=1).astype(BF16)
    time_vector = dot(features, time_ref[...])
    time_rows = jnp.where(iota((8, model), 0) == 0, time_vector, 0.0)
    copies[1].wait()
    basis = jnp.concatenate([patch_ref[...].astype(F32), time_rows], axis=0)
    basis = basis - jnp.mean(basis, axis=1, keepdims=True)

    gram = dot(basis, basis, 1, 1, lax.Precision.HIGHEST) * (1.0 / model)
    high, rest = split(gram)
    middle, rest = split(rest)
    gram_ref[...] = jnp.concatenate([high, middle, rest], axis=0).astype(BF16)

    copies[2].wait()
    average = dot(jnp.ones((8, model), BF16), toutput_ref[...], 1, 1)[:1] * (1.0 / model)
    high, rest = split(average)
    outt_ref[pl.ds(16, model), :] = toutput_ref[...].T
    outt_ref[pl.ds(0, 16), :] = jnp.concatenate(
        [high, rest, jnp.zeros((14, inner), F32)], axis=0
    ).astype(BF16)
    outt_copy = pltpu.make_async_copy(outt_ref, outt_hbm, sems.at[10])
    outt_copy.start()

    both = jnp.concatenate(split(basis), axis=0).astype(BF16)
    folded = []
    for k in range(3):
        copies[3 + k].wait()
        if k == 2:
            copies[6].wait()
        value = dot(both, sproject_ref[parts[k], :], 1, 1)
        folded.append(value[:BASIS] + value[BASIS:])
    queries, keys, values = folded
    def by_head(value, first, count):
        lane = iota(value.shape, 1)
        return [
            jnp.where((lane >= h * HEAD_DIM) & (lane < (h + 1) * HEAD_DIM), value, 0.0)
            for h in range(first, first + count)
        ]

    khigh, krest = (
        jnp.concatenate(by_head(v, 0, HEADS), axis=0).astype(BF16) for v in split(keys)
    )
    qhigh, qrest = split(queries * scale)
    both = dot(jnp.concatenate([qhigh, qrest], axis=0).astype(BF16), khigh, 1, 1)
    score = both[:BASIS] + both[BASIS:] + dot(qhigh.astype(BF16), krest, 1, 1)
    unused = jnp.zeros((LANES - BASIS, HEADS * BASIS), F32)
    high, rest = split(jnp.concatenate([score, unused], axis=0).T[:, :BASIS])
    score_ref[...] = jnp.concatenate([high, high, rest], axis=1).astype(BF16)

    group = 2 if (2 * HEAD_DIM) % 16 == 0 else HEADS
    mixed = []
    for first in range(0, HEADS, group):
        cut = slice(first * HEAD_DIM, (first + group) * HEAD_DIM)
        both = jnp.concatenate(
            [part for v in split(values[:, cut]) for part in by_head(v, 0, group)], axis=0
        )
        both = dot(both.astype(BF16), soutput_ref[cut, :])
        mixed.append(both[: group * BASIS] + both[group * BASIS :])
    mixed = jnp.concatenate(mixed, axis=0)
    mixed = mixed - jnp.mean(mixed, axis=1, keepdims=True)
    depth = mixt_ref.shape[1]
    used = (HEADS + 1) * BASIS
    whole = jnp.concatenate([basis, mixed, jnp.zeros((depth - used, model), F32)], axis=0)
    whole = whole.astype(BF16)
    mixt_ref[...] = whole.T

    folded = []
    for k, cut in enumerate(halves):
        copies[7 + k].wait()
        count = (cut.stop - cut.start) // 2
        for start in (cut.start, cut.start + count):
            folded.append(dot(tproject_ref[pl.ds(start, count), :], whole, 1, 1))
    folded = jnp.concatenate(folded, axis=0)
    queries, keys, values = (folded[cut] for cut in parts)
    mark = iota((LANES - HEAD_DIM, depth), 1) - used
    row = iota((LANES - HEAD_DIM, depth), 0)
    placed = (mark >= 0) & (mark < low) & (row < low)
    key_mark = jnp.where(placed & (mark == row), 1.0, 0.0)
    query_mark = jnp.where(placed & (mark != row), -1e30, 0.0)[: plan.qpad - HEAD_DIM]
    blank = jnp.zeros((VPAD - HEAD_DIM, depth), F32)
    padded = []
    for h in range(HEADS):
        cut = slice(h * HEAD_DIM, (h + 1) * HEAD_DIM)
        padded += [keys[cut], key_mark]
        query_ref[pl.ds(h * plan.qpad, plan.qpad), :] = jnp.concatenate(
            [queries[cut] * scale, query_mark], axis=0
        ).astype(BF16)
        value_ref[pl.ds(h * VPAD, VPAD), :] = jnp.concatenate(
            [values[cut], blank], axis=0
        ).astype(BF16)
    key_ref[...] = jnp.concatenate(padded, axis=0).astype(BF16).T
    outt_copy.wait()


def main_kernel(
    plan,
    recv_ref,
    gram_ref,
    score_ref,
    mixt_ref,
    query_ref,
    key_ref,
    value_ref,
    outt_hbm,
    order_ref,
    rows_ref,
    finalt_ref,
    out_ref,
    mixed_ref,
    stream_ref,
    outt_ref,
    total_ref,
    sem,
):
    window, places, tokens = plan.window, plan.places, plan.tokens
    frames, stride = plan.frames, plan.stride
    channels = recv_ref.shape[1]
    depth = mixt_ref.shape[1]
    used = (HEADS + 1) * BASIS

    outt_copy = pltpu.make_async_copy(outt_hbm, outt_ref, sem)
    outt_copy.start()
    groups = range(places // plan.low)
    order = cat(
        [order_ref[pl.ds((len(groups) - 1 - k) * plan.low, tokens), :] for k in groups], 1
    )

    def add(f, carry):
        value = recv_ref[f * plan.halves].astype(F32)
        for r in range(1, plan.halves):
            value = value + recv_ref[f * plan.halves + r].astype(F32)
        total_ref[f] = value
        return carry

    lax.fori_loop(0, frames, add, 0)
    received = [total_ref[f] for f in range(frames)]

    def query_lanes(values, k=0):
        return cat([v[:, window + k * places : window + (k + 1) * places] for v in values], 1)

    ones = (iota((BASIS - channels, frames * stride), 0) == 0).astype(F32)
    basis = jnp.concatenate([cat([v[:, :stride] for v in received], 1), ones], axis=0)
    image = dot(gram_ref[...], basis.astype(BF16))
    image = image[:BASIS] + image[BASIS : 2 * BASIS] + image[2 * BASIS :]
    variance = jnp.sum(basis * image, axis=0, keepdims=True)
    scaled = basis * lax.rsqrt(jnp.maximum(variance, 0.0) + EPS)
    high, rest = split(scaled)
    by_frame = [slice(f * stride, (f + 1) * stride) for f in range(frames)]
    qhigh, qrest = (query_lanes([v[:, cut] for cut in by_frame]) for v in (high, rest))
    turned = dot(score_ref[...], jnp.concatenate([qhigh, qrest, qhigh], axis=0).astype(BF16))
    qhigh, qrest = split(turned)

    packed = min(HEADS, 2 * LANES // places)
    sides = cat([rows_ref[...]] * (packed * places // LANES), 1)
    starts = range(0, HEADS, packed)
    key_row = jnp.zeros((plan.marks, stride), jnp.int32)
    for k in range(1, window // plan.cols):
        key_row = key_row + (iota((plan.marks, stride), 1) >= k * plan.cols).astype(jnp.int32)
    marks = (iota((plan.marks, stride), 0) == key_row).astype(F32)
    count = (iota((8, window), 0) == 0).astype(F32)

    def gather(value, f, start):
        return cat(
            [
                value[h * BASIS : (h + 1) * BASIS, f * places : (f + 1) * places]
                for h in range(start, start + packed)
            ],
            1,
        )

    scores, lefts = [], []
    for f in range(frames):
        fhigh, frest = high[:, by_frame[f]], rest[:, by_frame[f]]
        left = jnp.concatenate([fhigh, fhigh, frest, marks], axis=0).T.astype(BF16)[:window]
        lefts.append(
            jnp.concatenate([fhigh[:, :window], frest[:, :window], count], axis=0).astype(BF16)
        )
        for start in starts:
            ahigh, arest = gather(qhigh, f, start), gather(qrest, f, start)
            right = jnp.concatenate([ahigh, arest, ahigh, sides], axis=0)
            scores.append(dot(left, right.astype(BF16)))
    weights = [
        jnp.exp2(score - jnp.max(score, axis=0, keepdims=True)).astype(BF16)
        for score in scores
    ]
    pieces = [[None] * frames for _ in range(HEADS)]
    for n, weight in enumerate(weights):
        f, start = n // len(starts), (n % len(starts)) * packed
        sums = dot(lefts[f], weight)
        inverse = 1.0 / sums[2 * BASIS : 2 * BASIS + 1]
        mean = (sums[:BASIS] + sums[BASIS : 2 * BASIS]) * inverse
        for k in range(packed):
            pieces[start + k][f] = mean[:, k * places : (k + 1) * places]
    own = jnp.concatenate([query_lanes(received), ones[:, :tokens]], axis=0)
    combined = jnp.concatenate(
        [own]
        + [cat(piece, 1) for piece in pieces]
        + [jnp.zeros((depth - used, tokens), F32)]
        + [query_lanes(received, k) for k in (1, 2)],
        axis=0,
    ).astype(BF16)
    combined = dot(combined, order)
    noise = combined[depth : depth + channels] + combined[depth + channels :]
    combined = combined[:depth]

    stream = dot(mixt_ref[...], combined.astype(BF16))
    stream_ref[...] = stream
    variance = jnp.mean(stream * stream, axis=0, keepdims=True)
    placed = (iota((depth - used, tokens), 1) & (plan.low - 1)) == iota((depth - used, tokens), 0)
    combined = jnp.concatenate(
        [combined[:used] * lax.rsqrt(variance + EPS), placed.astype(F32)], axis=0
    ).astype(BF16)
    keys = dot(combined, key_ref[...], 0, 0).astype(BF16)
    queries = dot(query_ref[...], combined).astype(BF16)
    values = dot(value_ref[...], combined).astype(BF16)
    units = [(slice(g, g + LANES), h) for g in range(0, tokens, LANES) for h in range(HEADS)]
    scores = [
        dot(
            keys[cut, h * LANES : h * LANES + plan.qpad],
            queries[h * plan.qpad : (h + 1) * plan.qpad, cut],
        )
        for cut, h in units
    ]
    weights, totals = [], []
    for score in scores:
        weight = jnp.exp2(score - jnp.max(score, axis=0, keepdims=True))
        totals.append(jnp.sum(weight, axis=0, keepdims=True))
        weights.append(weight.astype(BF16))
    for (cut, h), weight, total in zip(units, weights, totals):
        mean = dot(values[h * VPAD : (h + 1) * VPAD, cut], weight) * (1.0 / total)
        mixed_ref[pl.ds(h * HEAD_DIM, HEAD_DIM), cut] = mean[:HEAD_DIM]

    outt_copy.wait()
    delta = dot(outt_ref[...], mixed_ref[...].astype(BF16))
    average = delta[:1] + delta[1:2]
    stream = (stream_ref[...] - average) + delta[16:]
    variance = jnp.mean(stream * stream, axis=0, keepdims=True)
    predicted = dot(finalt_ref[...], stream.astype(BF16)) * lax.rsqrt(variance + EPS)
    gap = predicted - noise
    errors = jnp.mean(gap * gap, axis=0, keepdims=True)
    high, rest = split(errors)
    middle, rest = split(rest)
    parts = jnp.concatenate([high, middle, rest] + [jnp.zeros_like(rest)] * 5, axis=0)
    errors = jnp.sum(dot(parts.astype(BF16), order, 1, 1), axis=0, keepdims=True)
    lanes = out_ref.shape[1]
    for k in range(tokens // lanes):
        out_ref[pl.ds(k, 1), :] = errors[:, k * lanes : (k + 1) * lanes]


def grant(mib):
    return pltpu.CompilerParams(vmem_limit_bytes=mib << 20)


def near(value):
    return pltpu.with_memory_space_constraint(value, pltpu.VMEM)


def far(value):
    return pltpu.with_memory_space_constraint(value, pltpu.HBM)


def local(
    latents,
    target_noise,
    timesteps,
    patch_weight,
    time_weight,
    spatial_project,
    spatial_output,
    temporal_project,
    temporal_output,
    final_weight,
):
    videos, _, rows, cols, channels = latents.shape
    frames, halves = lax.axis_size("frame"), lax.axis_size("row")
    plan = Plan(videos, rows, cols, frames, halves)
    inner, model = spatial_output.shape
    depth = -(-(HEADS + 1) * BASIS // LANES) * LANES
    shape = jax.ShapeDtypeStruct

    def by_row(value):
        return value.reshape(videos, rows, cols, channels).transpose(0, 1, 3, 2)

    send, time_near = pl.pallas_call(
        functools.partial(pack_kernel, plan),
        out_shape=(
            pltpu.VMEM((frames * halves, channels, plan.width), BF16),
            pltpu.VMEM(time_weight.shape, time_weight.dtype),
        ),
        in_specs=[HBM] * 4,
        out_specs=(VMEM,) * 2,
        compiler_params=grant(26),
        scratch_shapes=[
            pltpu.SMEM(timesteps.shape, timesteps.dtype),
            pltpu.VMEM((videos, rows, channels, cols), F32),
            pltpu.VMEM((videos, rows, channels, cols), F32),
            pltpu.SemaphoreType.DMA((4,)),
        ],
    )(*map(far, (timesteps, by_row(latents), by_row(target_noise), time_weight)))
    received = lax.all_to_all(send, ("frame", "row"), 0, 0, tiled=True)

    weights = (
        patch_weight,
        spatial_project.T,
        spatial_output,
        temporal_project.T,
        temporal_output,
    )
    tables = pl.pallas_call(
        functools.partial(fold_kernel, plan),
        out_shape=(
            pltpu.VMEM((3 * BASIS, BASIS), BF16),
            pltpu.VMEM((HEADS * BASIS, 3 * BASIS), BF16),
            pltpu.VMEM((model, depth), BF16),
            pltpu.VMEM((HEADS * plan.qpad, depth), BF16),
            pltpu.VMEM((depth, HEADS * LANES), BF16),
            pltpu.VMEM((HEADS * VPAD, depth), BF16),
            pltpu.HBM((model + 16, inner), BF16),
            pltpu.VMEM((plan.tokens + plan.places - plan.low, LANES), BF16),
            pltpu.VMEM((plan.marks, LANES), F32),
        ),
        in_specs=[VMEM] + [HBM] * (1 + len(weights)),
        out_specs=(VMEM,) * 6 + (HBM,) + (VMEM,) * 2,
        scratch_shapes=[pltpu.SMEM(timesteps.shape, timesteps.dtype)]
        + [pltpu.VMEM(w.shape, w.dtype) for w in weights]
        + [pltpu.VMEM((model + 16, inner), BF16), pltpu.SemaphoreType.DMA((11,))],
        compiler_params=grant(26),
    )(near(time_near), *map(far, (timesteps, *weights)))

    outt = tables[6]
    lanes = min(plan.places, cols)
    errors = pl.pallas_call(
        functools.partial(main_kernel, plan),
        out_shape=shape((plan.tokens // lanes, lanes), F32),
        in_specs=[VMEM] * 7 + [HBM] + [VMEM] * 3,
        out_specs=VMEM,
        compiler_params=grant(26),
        scratch_shapes=[
            pltpu.VMEM((inner, plan.tokens), F32),
            pltpu.VMEM((model, plan.tokens), F32),
            pltpu.VMEM(outt.shape, outt.dtype),
            pltpu.VMEM((frames, channels, plan.width), F32),
            pltpu.SemaphoreType.DMA,
        ],
    )(
        *map(near, (received, *tables[:6])),
        far(outt),
        *map(near, (*tables[7:], final_weight.T)),
    )
    errors = lax.all_to_all(errors, "frame", 0, 0, tiled=True)
    return errors.reshape(videos, 1, rows, cols)


def solution(mesh):
    return jax.shard_map(
        local,
        mesh=mesh,
        in_specs=(
            P("grp", "frame", "row", None, None),
            P("grp", "frame", "row", None, None),
            P("grp"),
            P(),
            P(),
            P(),
            P(),
            P(),
            P(),
            P(),
        ),
        out_specs=P("grp", "frame", "row", None),
        check_vma=False,
    )
```

```python
import functools
import math

import jax
import jax.numpy as jnp
from jax import lax
from jax.experimental import pallas as pl
from jax.experimental.pallas import tpu as pltpu
from jax.sharding import PartitionSpec as P

HEAD_DIM = 72
HEADS = 8
STEPS = 1000
REACH = 2
EPS = 1e-06
LANES = 128
BASIS = 24
VPAD = 80
F32 = jnp.float32
BF16 = jnp.bfloat16
VMEM = pl.BlockSpec(memory_space=pltpu.VMEM)
SMEM = pl.BlockSpec(memory_space=pltpu.SMEM)
HBM = pl.BlockSpec(memory_space=pltpu.HBM)


def dot(a, b, ca=1, cb=0, precision=None):
    return lax.dot_general(
        a, b, (((ca,), (cb,)), ((), ())), preferred_element_type=F32, precision=precision
    )


def split(x):
    high = x.astype(BF16).astype(F32)
    return high, x - high


def iota(shape, dim):
    return lax.broadcasted_iota(jnp.int32, shape, dim)


def cat(parts, axis):
    return parts[0] if len(parts) == 1 else jnp.concatenate(parts, axis=axis)


class Plan:
    def __init__(self, videos, rows, cols, frames, halves):
        self.videos, self.rows, self.cols = videos, rows, cols
        self.frames, self.halves = frames, halves
        self.chunks = frames // videos
        self.places = rows * cols // self.chunks
        self.qrows = max(1, self.places // cols)
        self.window = (self.qrows + 2 * REACH) * cols
        self.width = -(-(self.window + 3 * self.places) // LANES) * LANES
        self.tokens = frames * self.places
        self.low = LANES // frames
        self.stride = -(-(self.window + self.places) // LANES) * LANES
        self.marks = -(-(self.qrows + 2 * REACH) // 8) * 8
        self.qpad = -(-(HEAD_DIM + self.low) // 16) * 16
        whole = self.qrows * cols if self.places >= cols else cols
        assert frames % videos == 0 and (rows * cols) % self.chunks == 0
        assert self.places % cols == 0 or cols % self.places == 0
        assert rows >= REACH and rows % self.qrows == 0 and whole >= self.places
        for size in (cols, frames, self.places, self.low):
            assert size & (size - 1) == 0 and size > 0
        assert self.places % self.low == 0 and self.tokens % LANES == 0


def log_kept(step):
    counter = iota((8, LANES), 0) * LANES + iota((8, LANES), 1)
    beta = 0.0001 + (0.02 - 0.0001) * counter.astype(F32) / (STEPS - 1)
    used = (counter <= step) & (counter < STEPS)
    terms = jnp.where(used, jnp.log1p(-jnp.where(used, beta, 0.0)), 0.0)
    return jnp.sum(jnp.sum(terms, axis=0, keepdims=True), axis=1, keepdims=True)


def pack_kernel(
    plan,
    steps_hbm,
    latents_hbm,
    noise_hbm,
    time_hbm,
    send_ref,
    time_ref,
    steps_ref,
    latents_ref,
    noise_ref,
    sems,
):
    pairs = [(steps_hbm, steps_ref), (latents_hbm, latents_ref), (noise_hbm, noise_ref)]
    pairs += [(time_hbm, time_ref)]
    copies = [
        pltpu.make_async_copy(source, target, sems.at[k])
        for k, (source, target) in enumerate(pairs)
    ]
    for copy in copies:
        copy.start()
    for copy in copies[:3]:
        copy.wait()
    half = lax.axis_index("row")
    channels = latents_ref.shape[2]
    videos = []
    for video in range(plan.videos):
        kept = jnp.exp(log_kept(steps_ref[video]))
        signal, spread = jnp.sqrt(kept), jnp.sqrt(1.0 - kept)
        noise = cat([noise_ref[video, row] for row in range(plan.rows)], 1)
        clean = cat([latents_ref[video, row] for row in range(plan.rows)], 1)
        videos.append((signal * clean + spread * noise, *split(noise)))

    def window(value, start, count):
        first, last = max(start, 0), min(start + count, plan.rows)
        if first >= last:
            return jnp.zeros((channels, count * plan.cols), F32)
        parts = []
        if first > start:
            parts.append(jnp.zeros((channels, (first - start) * plan.cols), F32))
        parts.append(value[:, first * plan.cols : last * plan.cols])
        if last < start + count:
            parts.append(jnp.zeros((channels, (start + count - last) * plan.cols), F32))
        return cat(parts, 1)

    unused = plan.width - plan.window - 3 * plan.places
    for target in range(plan.halves):
        for apart in range(1 - plan.halves, plan.halves):
            if not 0 <= target + apart < plan.halves:
                continue

            @pl.when(half == target + apart)
            def _():
                for peer in range(plan.frames):
                    values = videos[peer // plan.chunks]
                    place = (peer % plan.chunks) * plan.places
                    start = place // plan.cols - REACH - apart * plan.rows
                    parts = [window(values[0], start, plan.qrows + 2 * REACH)]
                    if apart == 0:
                        parts += [v[:, place : place + plan.places] for v in values]
                        if unused:
                            parts.append(jnp.zeros((channels, unused), F32))
                    else:
                        parts.append(jnp.zeros((channels, plan.width - plan.window), F32))
                    send_ref[peer * plan.halves + target] = cat(parts, 1).astype(BF16)
    copies[3].wait()


def fold_kernel(
    plan,
    time_ref,
    steps_hbm,
    patch_hbm,
    sproject_hbm,
    soutput_hbm,
    tproject_hbm,
    toutput_hbm,
    gram_ref,
    score_ref,
    mixt_ref,
    query_ref,
    key_ref,
    value_ref,
    outt_hbm,
    order_ref,
    rows_ref,
    steps_ref,
    patch_ref,
    sproject_ref,
    soutput_ref,
    tproject_ref,
    toutput_ref,
    outt_ref,
    sems,
):
    model = patch_ref.shape[1]
    inner = soutput_ref.shape[0]
    halfway = time_ref.shape[0] // 2
    tokens, places, low = plan.tokens, plan.places, plan.low
    scale = math.log2(math.e) / math.sqrt(HEAD_DIM)
    parts = [slice(k * inner, (k + 1) * inner) for k in range(3)]
    pairs = [(steps_hbm, steps_ref), (patch_hbm, patch_ref), (toutput_hbm, toutput_ref)]
    pairs += [(sproject_hbm.at[cut], sproject_ref.at[cut]) for cut in parts]
    pairs += [(soutput_hbm, soutput_ref)]
    total = 3 * inner
    halves = [slice(0, total // 2), slice(total // 2, total)]
    pairs += [(tproject_hbm.at[cut], tproject_ref.at[cut]) for cut in halves]
    copies = [
        pltpu.make_async_copy(source, target, sems.at[k])
        for k, (source, target) in enumerate(pairs)
    ]
    for copy in copies:
        copy.start()

    lane = iota(order_ref.shape, 1)
    row = iota(order_ref.shape, 0) - (places // low - 1) * low
    order_ref[...] = (row == (lane // low) * places + (lane & (low - 1))).astype(BF16)

    half = lax.axis_index("row")
    chunk = lax.rem(lax.axis_index("frame"), plan.chunks)
    top = half * plan.rows + lax.div(chunk * places, plan.cols) - REACH
    key_row = iota((plan.marks, LANES), 0)
    query = iota((plan.marks, LANES), 1) & (places - 1)
    query_row = jnp.zeros((plan.marks, LANES), jnp.int32)
    for k in range(1, plan.qrows):
        query_row = query_row + (query >= k * plan.cols).astype(jnp.int32)
    seen = (key_row >= query_row) & (key_row <= query_row + 2 * REACH)
    seen = seen & (key_row + top >= 0) & (key_row + top < plan.halves * plan.rows)
    rows_ref[...] = jnp.where(seen, 0.0, -1e30)

    copies[0].wait()
    step = steps_ref[lax.axis_index("frame") // plan.chunks]
    freqs = jnp.exp(iota((8, halfway), 1).astype(F32) * (-math.log(10000.0) / halfway))
    angles = step.astype(F32) * freqs
    features = jnp.concatenate([jnp.cos(angles), jnp.sin(angles)], axis=1).astype(BF16)
    time_vector = dot(features, time_ref[...])
    time_rows = jnp.where(iota((8, model), 0) == 0, time_vector, 0.0)
    copies[1].wait()
    basis = jnp.concatenate([patch_ref[...].astype(F32), time_rows], axis=0)
    basis = basis - jnp.mean(basis, axis=1, keepdims=True)

    gram = dot(basis, basis, 1, 1, lax.Precision.HIGHEST) * (1.0 / model)
    high, rest = split(gram)
    middle, rest = split(rest)
    gram_ref[...] = jnp.concatenate([high, middle, rest], axis=0).astype(BF16)

    copies[2].wait()
    average = dot(jnp.ones((8, model), BF16), toutput_ref[...], 1, 1)[:1] * (1.0 / model)
    high, rest = split(average)
    outt_ref[pl.ds(16, model), :] = toutput_ref[...].T
    outt_ref[pl.ds(0, 16), :] = jnp.concatenate(
        [high, rest, jnp.zeros((14, inner), F32)], axis=0
    ).astype(BF16)
    outt_copy = pltpu.make_async_copy(outt_ref, outt_hbm, sems.at[10])
    outt_copy.start()

    both = jnp.concatenate(split(basis), axis=0).astype(BF16)
    folded = []
    for k in range(3):
        copies[3 + k].wait()
        if k == 2:
            copies[6].wait()
        value = dot(both, sproject_ref[parts[k], :], 1, 1)
        folded.append(value[:BASIS] + value[BASIS:])
    queries, keys, values = folded
    def by_head(value, first, count):
        lane = iota(value.shape, 1)
        return [
            jnp.where((lane >= h * HEAD_DIM) & (lane < (h + 1) * HEAD_DIM), value, 0.0)
            for h in range(first, first + count)
        ]

    khigh, krest = (
        jnp.concatenate(by_head(v, 0, HEADS), axis=0).astype(BF16) for v in split(keys)
    )
    qhigh, qrest = split(queries * scale)
    both = dot(jnp.concatenate([qhigh, qrest], axis=0).astype(BF16), khigh, 1, 1)
    score = both[:BASIS] + both[BASIS:] + dot(qhigh.astype(BF16), krest, 1, 1)
    unused = jnp.zeros((LANES - BASIS, HEADS * BASIS), F32)
    high, rest = split(jnp.concatenate([score, unused], axis=0).T[:, :BASIS])
    score_ref[...] = jnp.concatenate([high, high, rest], axis=1).astype(BF16)

    group = 2 if (2 * HEAD_DIM) % 16 == 0 else HEADS
    mixed = []
    for first in range(0, HEADS, group):
        cut = slice(first * HEAD_DIM, (first + group) * HEAD_DIM)
        both = jnp.concatenate(
            [part for v in split(values[:, cut]) for part in by_head(v, 0, group)], axis=0
        )
        both = dot(both.astype(BF16), soutput_ref[cut, :])
        mixed.append(both[: group * BASIS] + both[group * BASIS :])
    mixed = jnp.concatenate(mixed, axis=0)
    mixed = mixed - jnp.mean(mixed, axis=1, keepdims=True)
    depth = mixt_ref.shape[1]
    used = (HEADS + 1) * BASIS
    whole = jnp.concatenate([basis, mixed, jnp.zeros((depth - used, model), F32)], axis=0)
    whole = whole.astype(BF16)
    mixt_ref[...] = whole.T

    folded = []
    for k, cut in enumerate(halves):
        copies[7 + k].wait()
        count = (cut.stop - cut.start) // 2
        for start in (cut.start, cut.start + count):
            folded.append(dot(tproject_ref[pl.ds(start, count), :], whole, 1, 1))
    folded = jnp.concatenate(folded, axis=0)
    queries, keys, values = (folded[cut] for cut in parts)
    mark = iota((LANES - HEAD_DIM, depth), 1) - used
    row = iota((LANES - HEAD_DIM, depth), 0)
    placed = (mark >= 0) & (mark < low) & (row < low)
    key_mark = jnp.where(placed & (mark == row), 1.0, 0.0)
    query_mark = jnp.where(placed & (mark != row), -1e30, 0.0)[: plan.qpad - HEAD_DIM]
    blank = jnp.zeros((VPAD - HEAD_DIM, depth), F32)
    padded = []
    for h in range(HEADS):
        cut = slice(h * HEAD_DIM, (h + 1) * HEAD_DIM)
        padded += [keys[cut], key_mark]
        query_ref[pl.ds(h * plan.qpad, plan.qpad), :] = jnp.concatenate(
            [queries[cut] * scale, query_mark], axis=0
        ).astype(BF16)
        value_ref[pl.ds(h * VPAD, VPAD), :] = jnp.concatenate(
            [values[cut], blank], axis=0
        ).astype(BF16)
    key_ref[...] = jnp.concatenate(padded, axis=0).astype(BF16).T
    outt_copy.wait()


def main_kernel(
    plan,
    recv_ref,
    gram_ref,
    score_ref,
    mixt_ref,
    query_ref,
    key_ref,
    value_ref,
    outt_hbm,
    order_ref,
    rows_ref,
    finalt_ref,
    out_ref,
    mixed_ref,
    stream_ref,
    outt_ref,
    total_ref,
    sem,
):
    window, places, tokens = plan.window, plan.places, plan.tokens
    frames, stride = plan.frames, plan.stride
    channels = recv_ref.shape[1]
    depth = mixt_ref.shape[1]
    used = (HEADS + 1) * BASIS

    outt_copy = pltpu.make_async_copy(outt_hbm, outt_ref, sem)
    outt_copy.start()
    groups = range(places // plan.low)
    order = cat(
        [order_ref[pl.ds((len(groups) - 1 - k) * plan.low, tokens), :] for k in groups], 1
    )

    step = max(1, frames // 2)

    def add(k, carry):
        for n in range(step):
            f = k * step + n
            value = recv_ref[f * plan.halves].astype(F32)
            for r in range(1, plan.halves):
                value = value + recv_ref[f * plan.halves + r].astype(F32)
            total_ref[f] = value
        return carry

    lax.fori_loop(0, frames // step, add, 0)
    received = [total_ref[f] for f in range(frames)]

    def query_lanes(values, k=0):
        return cat([v[:, window + k * places : window + (k + 1) * places] for v in values], 1)

    ones = (iota((BASIS - channels, frames * stride), 0) == 0).astype(F32)
    basis = jnp.concatenate([cat([v[:, :stride] for v in received], 1), ones], axis=0)
    image = dot(gram_ref[...], basis.astype(BF16))
    image = image[:BASIS] + image[BASIS : 2 * BASIS] + image[2 * BASIS :]
    variance = jnp.sum(basis * image, axis=0, keepdims=True)
    scaled = basis * lax.rsqrt(jnp.maximum(variance, 0.0) + EPS)
    high, rest = split(scaled)
    by_frame = [slice(f * stride, (f + 1) * stride) for f in range(frames)]
    qhigh, qrest = (query_lanes([v[:, cut] for cut in by_frame]) for v in (high, rest))
    turned = dot(score_ref[...], jnp.concatenate([qhigh, qrest, qhigh], axis=0).astype(BF16))
    qhigh, qrest = split(turned)

    packed = min(HEADS, 2 * LANES // places)
    sides = cat([rows_ref[...]] * (packed * places // LANES), 1)
    starts = range(0, HEADS, packed)
    key_row = jnp.zeros((plan.marks, stride), jnp.int32)
    for k in range(1, window // plan.cols):
        key_row = key_row + (iota((plan.marks, stride), 1) >= k * plan.cols).astype(jnp.int32)
    marks = (iota((plan.marks, stride), 0) == key_row).astype(F32)
    count = (iota((8, window), 0) == 0).astype(F32)

    def gather(value, f, start):
        return cat(
            [
                value[h * BASIS : (h + 1) * BASIS, f * places : (f + 1) * places]
                for h in range(start, start + packed)
            ],
            1,
        )

    scores, lefts = [], []
    for f in range(frames):
        fhigh, frest = high[:, by_frame[f]], rest[:, by_frame[f]]
        left = jnp.concatenate([fhigh, fhigh, frest, marks], axis=0).T.astype(BF16)[:window]
        lefts.append(
            jnp.concatenate([fhigh[:, :window], frest[:, :window], count], axis=0).astype(BF16)
        )
        for start in starts:
            ahigh, arest = gather(qhigh, f, start), gather(qrest, f, start)
            right = jnp.concatenate([ahigh, arest, ahigh, sides], axis=0)
            scores.append(dot(left, right.astype(BF16)))
    weights = [
        jnp.exp2(score - jnp.max(score, axis=0, keepdims=True)).astype(BF16)
        for score in scores
    ]
    pieces = [[None] * frames for _ in range(HEADS)]
    for n, weight in enumerate(weights):
        f, start = n // len(starts), (n % len(starts)) * packed
        sums = dot(lefts[f], weight)
        inverse = 1.0 / sums[2 * BASIS : 2 * BASIS + 1]
        mean = (sums[:BASIS] + sums[BASIS : 2 * BASIS]) * inverse
        for k in range(packed):
            pieces[start + k][f] = mean[:, k * places : (k + 1) * places]
    own = jnp.concatenate([query_lanes(received), ones[:, :tokens]], axis=0)
    combined = jnp.concatenate(
        [own]
        + [cat(piece, 1) for piece in pieces]
        + [jnp.zeros((depth - used, tokens), F32)]
        + [query_lanes(received, k) for k in (1, 2)],
        axis=0,
    ).astype(BF16)
    combined = dot(combined, order)
    noise = combined[depth : depth + channels] + combined[depth + channels :]
    combined = combined[:depth]

    stream = dot(mixt_ref[...], combined.astype(BF16))
    stream_ref[...] = stream
    variance = jnp.mean(stream * stream, axis=0, keepdims=True)
    placed = (iota((depth - used, tokens), 1) & (plan.low - 1)) == iota((depth - used, tokens), 0)
    combined = jnp.concatenate(
        [combined[:used] * lax.rsqrt(variance + EPS), placed.astype(F32)], axis=0
    ).astype(BF16)
    keys = dot(combined, key_ref[...], 0, 0).astype(BF16)
    queries = dot(query_ref[...], combined).astype(BF16)
    values = dot(value_ref[...], combined).astype(BF16)
    units = [(slice(g, g + LANES), h) for g in range(0, tokens, LANES) for h in range(HEADS)]
    scores = [
        dot(
            keys[cut, h * LANES : h * LANES + plan.qpad],
            queries[h * plan.qpad : (h + 1) * plan.qpad, cut],
        )
        for cut, h in units
    ]
    weights, totals = [], []
    for score in scores:
        weight = jnp.exp2(score - jnp.max(score, axis=0, keepdims=True))
        totals.append(jnp.sum(weight, axis=0, keepdims=True))
        weights.append(weight.astype(BF16))
    for (cut, h), weight, total in zip(units, weights, totals):
        mean = dot(values[h * VPAD : (h + 1) * VPAD, cut], weight) * (1.0 / total)
        mixed_ref[pl.ds(h * HEAD_DIM, HEAD_DIM), cut] = mean[:HEAD_DIM]

    outt_copy.wait()
    delta = dot(outt_ref[...], mixed_ref[...].astype(BF16))
    average = delta[:1] + delta[1:2]
    stream = (stream_ref[...] - average) + delta[16:]
    variance = jnp.mean(stream * stream, axis=0, keepdims=True)
    predicted = dot(finalt_ref[...], stream.astype(BF16)) * lax.rsqrt(variance + EPS)
    gap = predicted - noise
    errors = jnp.mean(gap * gap, axis=0, keepdims=True)
    high, rest = split(errors)
    middle, rest = split(rest)
    parts = jnp.concatenate([high, middle, rest] + [jnp.zeros_like(rest)] * 5, axis=0)
    errors = jnp.sum(dot(parts.astype(BF16), order, 1, 1), axis=0, keepdims=True)
    lanes = out_ref.shape[1]
    for k in range(tokens // lanes):
        out_ref[pl.ds(k, 1), :] = errors[:, k * lanes : (k + 1) * lanes]


def grant(mib):
    return pltpu.CompilerParams(
        vmem_limit_bytes=mib << 20
    )


def near(value):
    return pltpu.with_memory_space_constraint(value, pltpu.VMEM)


def far(value):
    return pltpu.with_memory_space_constraint(value, pltpu.HBM)


def local(
    latents,
    target_noise,
    timesteps,
    patch_weight,
    time_weight,
    spatial_project,
    spatial_output,
    temporal_project,
    temporal_output,
    final_weight,
):
    videos, _, rows, cols, channels = latents.shape
    frames, halves = lax.axis_size("frame"), lax.axis_size("row")
    plan = Plan(videos, rows, cols, frames, halves)
    inner, model = spatial_output.shape
    depth = -(-(HEADS + 1) * BASIS // LANES) * LANES
    shape = jax.ShapeDtypeStruct

    def by_row(value):
        return value.reshape(videos, rows, cols, channels).transpose(0, 1, 3, 2)

    send, time_near = pl.pallas_call(
        functools.partial(pack_kernel, plan),
        out_shape=(
            pltpu.VMEM((frames * halves, channels, plan.width), BF16),
            pltpu.VMEM(time_weight.shape, time_weight.dtype),
        ),
        in_specs=[HBM] * 4,
        out_specs=(VMEM,) * 2,
        compiler_params=grant(26),
        scratch_shapes=[
            pltpu.SMEM(timesteps.shape, timesteps.dtype),
            pltpu.VMEM((videos, rows, channels, cols), F32),
            pltpu.VMEM((videos, rows, channels, cols), F32),
            pltpu.SemaphoreType.DMA((4,)),
        ],
    )(*map(far, (timesteps, by_row(latents), by_row(target_noise), time_weight)))
    received = lax.all_to_all(send, ("frame", "row"), 0, 0, tiled=True)

    weights = (
        patch_weight,
        spatial_project.T,
        spatial_output,
        temporal_project.T,
        temporal_output,
    )
    tables = pl.pallas_call(
        functools.partial(fold_kernel, plan),
        out_shape=(
            pltpu.VMEM((3 * BASIS, BASIS), BF16),
            pltpu.VMEM((HEADS * BASIS, 3 * BASIS), BF16),
            pltpu.VMEM((model, depth), BF16),
            pltpu.VMEM((HEADS * plan.qpad, depth), BF16),
            pltpu.VMEM((depth, HEADS * LANES), BF16),
            pltpu.VMEM((HEADS * VPAD, depth), BF16),
            pltpu.HBM((model + 16, inner), BF16),
            pltpu.VMEM((plan.tokens + plan.places - plan.low, LANES), BF16),
            pltpu.VMEM((plan.marks, LANES), F32),
        ),
        in_specs=[VMEM] + [HBM] * (1 + len(weights)),
        out_specs=(VMEM,) * 6 + (HBM,) + (VMEM,) * 2,
        scratch_shapes=[pltpu.SMEM(timesteps.shape, timesteps.dtype)]
        + [pltpu.VMEM(w.shape, w.dtype) for w in weights]
        + [pltpu.VMEM((model + 16, inner), BF16), pltpu.SemaphoreType.DMA((11,))],
        compiler_params=grant(26),
    )(near(time_near), *map(far, (timesteps, *weights)))

    outt = tables[6]
    lanes = min(plan.places, cols)
    errors = pl.pallas_call(
        functools.partial(main_kernel, plan),
        out_shape=shape((plan.tokens // lanes, lanes), F32),
        in_specs=[VMEM] * 7 + [HBM] + [VMEM] * 3,
        out_specs=VMEM,
        compiler_params=grant(26),
        scratch_shapes=[
            pltpu.VMEM((inner, plan.tokens), F32),
            pltpu.VMEM((model, plan.tokens), F32),
            pltpu.VMEM(outt.shape, outt.dtype),
            pltpu.VMEM((frames, channels, plan.width), F32),
            pltpu.SemaphoreType.DMA,
        ],
    )(
        *map(near, (received, *tables[:6])),
        far(outt),
        *map(near, (*tables[7:], final_weight.T)),
    )
    errors = lax.all_to_all(errors, "frame", 0, 0, tiled=True)
    return errors.reshape(videos, 1, rows, cols)


def solution(mesh):
    return jax.shard_map(
        local,
        mesh=mesh,
        in_specs=(
            P("grp", "frame", "row", None, None),
            P("grp", "frame", "row", None, None),
            P("grp"),
            P(),
            P(),
            P(),
            P(),
            P(),
            P(),
            P(),
        ),
        out_specs=P("grp", "frame", "row", None),
        check_vma=False,
    )
```
